32 devices in a mesh: groups: 1, ctx: 16 (over z, y, x), exp: 2 (over core).
Axes of the slice: x: 2, y: 2, z: 4, core: 2. Of those that a mesh axis runs over, the one named last changes fastest.
Arguments:
- queries: bfloat16 [2048, 2048], P(('groups', 'ctx'), 'exp'), may hold values from -40 to 40
- key_rows: bfloat16 [2048, 256], P(('groups', 'ctx'), 'exp'), may hold values from -15 to 15
- value_rows: bfloat16 [2048, 256], P(('groups', 'ctx'), 'exp'), may hold values from -6 to 6
- hidden_in: bfloat16 [2048, 1024], P(('groups', 'ctx')), may hold values from -40 to 40
- out_proj: bfloat16 [2048, 1024], P('exp'), may hold values from -0.125 to 0.125
- norm_gain: float32 [1024], replicated, may hold values from 0.1 to 1.9
- expert_ids: int32 [2048, 8], P(('groups', 'ctx')), may hold values from 0 to 15, all different within a row; in each aligned block of 128 rows (0 to 127, 128 to 255, ...) at most 96 rows name the same one
- gate_scores: float32 [2048, 8], P(('groups', 'ctx')), may hold values from 0.05 to 1
- w_gate: bfloat16 [16, 1024, 384], P('ctx'), may hold values from -0.1875 to 0.1875
- w_up: bfloat16 [16, 1024, 384], P('ctx'), may hold values from -0.1875 to 0.1875
- w_down: bfloat16 [16, 384, 1024], P('ctx'), may hold values from -0.3125 to 0.3125
Outputs:
- layer_out: bfloat16 [2048, 1024], P(('groups', 'ctx'), 'exp')
The draws below stay inside these ranges and needn't reach their ends.
Inputs may be any that keep to these rules, and one draw needn't show every extreme that they name: `expert_ids`: each row names 8 different experts. No expert is named by more than 96 rows of one aligned block of 128 rows, a bound that some block reaches.
All inputs are finite; a program needn't handle non-finite values.
Results may differ from the reference program's by a relative error of at most 0.0035.
Values may be sent and summed in bfloat16 or wider, within the bound.
No kernel may reach another device: no remote copies, remote signals or barrier semaphores. Data moves between devices by JAX's collectives and lax.ppermute only.
A program may use at most 64 MiB of HBM per device.

```python
import math
import jax
import jax.numpy as jnp
import numpy as np
from jax import lax

D = 1024
HQ = 16
HK = 2
HD = 128
FF = 384
TOPK = 8
TOK_DEV = 128
S = 2048
EXPERTS = 16
CAP = 96
N_CTX = 16


def query_key_pair(key):
    parts = jax.random.split(jax.random.fold_in(key, 23), 2)
    query_all = 3.0 * jax.random.normal(parts[0], (S, HQ * HD), jnp.float32)
    key_all = jax.random.normal(parts[1], (S, HK * HD), jnp.float32)
    return (jnp.clip(query_all, -40.0, 40.0), jnp.clip(key_all, -15.0, 15.0))


def draw_queries(key, part):
    return query_key_pair(key)[0].astype(jnp.bfloat16)


def draw_key_rows(key, part):
    return query_key_pair(key)[1].astype(jnp.bfloat16)


def draw_hidden_in(key, part):
    parts = jax.random.split(jax.random.fold_in(key, 7), 3)
    row_scale = jnp.exp(jax.random.uniform(parts[0], (S, 1), jnp.float32, math.log(0.3), math.log(3.0)))
    ramp = jnp.exp(jnp.linspace(0.0, math.log(3.0), D)).astype(jnp.float32)
    col_scale = ramp[None, :] * jnp.exp(jax.random.uniform(parts[1], (1, D), jnp.float32, 0.0, math.log(3.0)))
    base = jax.random.normal(parts[2], (S, D), jnp.float32)
    return jnp.clip(base * row_scale * col_scale, -40.0, 40.0).astype(jnp.bfloat16)


def shard_levels(key, extent, cuts, smallest, largest):
    def one(position, blocks):
        draws = jax.random.uniform(jax.random.fold_in(jax.random.fold_in(key, 6), position), (blocks,), jnp.float32, smallest / len(cuts), largest / len(cuts))
        return jnp.repeat(jnp.exp(draws), extent[position] // blocks).reshape((-1,) + (1,) * (len(extent) - position - 1))

    level = one(*cuts[0])
    for cut in cuts[1:]:
        level = level * one(*cut)
    return level


def routed_block(own_key, own, number, rows, number_of, top, bound, slope):
    ranking = jax.random.permutation(own_key, number_of)
    heavy_load, usual = portions_of(number_of, rows * top, bound, slope, True), portions_of(number_of, rows * top, bound, slope, False)
    places = jnp.arange(number_of)

    def named(sizes, turn):
        used = int((sizes > 0).sum())
        fixed = max(1, used // 4)
        shifted = fixed + (places - fixed + turn * (used - fixed)) % max(1, number_of - fixed)
        return jnp.zeros((number_of,), jnp.int32).at[ranking[jnp.where(places < fixed, places, shifted)]].set(jnp.asarray(sizes, jnp.int32))

    sizes = jnp.where(number % 4 == 0, named(heavy_load, number // 4), named(usual, number - number // 4 - 1))
    mixed = jax.random.permutation(jax.random.fold_in(own, 3), number_of)
    donor, sink = mixed[0:number_of // 2 * 2:2], mixed[1:number_of // 2 * 2:2]
    margin = jnp.minimum(sizes[donor] - 1, bound - sizes[sink]) // 2
    margin = jnp.where((donor == ranking[0]) | (sink == ranking[0]) | (sizes[sink] == 0), 0, jnp.maximum(margin, 0))
    shifted = jax.random.randint(jax.random.fold_in(own, 4), (number_of // 2,), 0, 1 << 20) % (margin + 1)
    sizes = sizes.at[donor].add(-shifted).at[sink].add(shifted)
    labels = jnp.searchsorted(jnp.cumsum(sizes), jnp.arange(rows * top), side="right").astype(jnp.int32)
    grid = labels.reshape(top, rows).T
    grid = grid[jax.random.permutation(jax.random.fold_in(own, 1), rows)]
    turn = jax.random.randint(jax.random.fold_in(own, 2), (rows, 1), 0, top)
    return jnp.take_along_axis(grid, (jnp.arange(top)[None, :] + turn) % top, axis=1)


def portions_of(count, total, bound, skew, full):
    portions = [(1 << 20) // math.isqrt(rank ** skew) + 1 for rank in range(1, count + 1)]
    largest = bound if full else min(bound, max(-(-total // count), total * portions[0] // sum(portions)))
    least = 1 if total - largest >= count - 1 else 0
    holding, spare = [largest] + [least] * (count - 1), total - largest - least * (count - 1)
    while spare > 0:
        movable = [i for i in range(1, count) if holding[i] < largest] or [i for i in range(1, count) if holding[i] < bound]
        mass, budget = sum([portions[i] for i in movable]), spare
        for i in movable:
            addition = min(bound - holding[i], max(1, budget * portions[i] // mass), spare)
            holding[i] = holding[i] + addition
            spare = spare - addition
    return np.array(holding)


def scatter_about(own_key, extent, scale, limit, cuts=(), held_as=jnp.bfloat16):
    values = scale * jax.random.normal(own_key, extent, jnp.float32)
    if cuts:
        values = values * shard_levels(own_key, extent, cuts, -0.22, 0.18)
    return jnp.clip(values, -limit, limit).astype(held_as)


def setup_inputs(seed: int = 0, part: int = 0) -> dict:
    key_of = jax.random.split(jax.random.key(seed), 12)
    own_keys = jax.random.split(jax.random.fold_in(key_of[11], part), 12)
    queries = draw_queries(jax.random.fold_in(jax.random.fold_in(key_of[11], part), 71), part)
    key_rows = draw_key_rows(jax.random.fold_in(jax.random.fold_in(key_of[11], part), 71), part)
    value_rows = scatter_about(own_keys[2], (S, HK * HD), 1.0, 6.0, ((0, 16), (1, 2)))
    hidden_in = draw_hidden_in(jax.random.fold_in(jax.random.fold_in(key_of[11], part), 71), part)
    out_proj = scatter_about(key_of[4], (HQ * HD, D), (HQ * HD) ** -0.5, 0.125, ((0, 2),))
    norm_gain = jnp.clip(1.0 + 0.18 * jax.random.normal(key_of[5], (D,), jnp.float32), 0.1, 1.9)
    expert_ids_keys = jax.random.split(jax.random.fold_in(own_keys[6], 1), S // TOK_DEV)
    expert_ids_turns = jax.random.permutation(jax.random.fold_in(own_keys[6], 3), S // TOK_DEV)
    expert_ids = jax.vmap(lambda own, number: routed_block(jax.random.fold_in(own_keys[6], 2), own, number, TOK_DEV, EXPERTS, TOPK, CAP, 2))(expert_ids_keys, expert_ids_turns).reshape((S, TOPK))
    gate_scores = jnp.clip(0.05 + 0.95 * jax.random.uniform(own_keys[7], (S, TOPK), jnp.float32) ** shard_levels(own_keys[7], (S, TOPK), ((0, 16),), -0.2, 0.2), 0.05, 1.0)
    w_gate = scatter_about(key_of[8], (EXPERTS, D, FF), D ** -0.5, 0.1875, ((0, 16),))
    w_up = scatter_about(key_of[9], (EXPERTS, D, FF), D ** -0.5, 0.1875, ((0, 16),))
    w_down = scatter_about(key_of[10], (EXPERTS, FF, D), FF ** -0.5, 0.3125, ((0, 16),))
    return dict(queries=queries, key_rows=key_rows, value_rows=value_rows, hidden_in=hidden_in, out_proj=out_proj, norm_gain=norm_gain, expert_ids=expert_ids, gate_scores=gate_scores, w_gate=w_gate, w_up=w_up, w_down=w_down)


def attention(queries, key_rows, value_rows):
    group = HQ // HK
    width = math.gcd(S, 128)
    key_all = key_rows.astype(jnp.float32).reshape(S, HK, HD)
    value_all = value_rows.astype(jnp.float32).reshape(S, HK, HD)
    key_pos = jnp.arange(S, dtype=jnp.int32)

    def one_block(start):
        block = lax.dynamic_slice_in_dim(queries, start, width, 0).astype(jnp.float32)
        block = block.reshape(width, HK, group, HD)
        scores = jnp.einsum('bkgd,tkd->kgbt', block, key_all) * HD ** (-0.5)
        query_pos = start + jnp.arange(width, dtype=jnp.int32)
        allowed = key_pos[None, :] <= query_pos[:, None]
        scores = jnp.where(allowed, scores, -jnp.inf)
        peak = lax.optimization_barrier(jnp.max(scores, axis=-1, keepdims=True))
        weights = jnp.exp(scores - peak)
        total = lax.optimization_barrier(jnp.sum(weights, axis=-1))
        rounded = weights.astype(jnp.bfloat16).astype(jnp.float32)
        summed = jnp.einsum('kgbt,tkd->kgbd', rounded, value_all)
        output = summed / total[..., None]
        output = jnp.transpose(output, (2, 0, 1, 3)).reshape(width, HQ * HD)
        return output.astype(jnp.bfloat16)
    starts = jnp.arange(S // width, dtype=jnp.int32) * width
    return lax.map(one_block, starts).reshape(S, HQ * HD)

def experts_out(normed, expert_ids, gate_scores, w_gate, w_up, w_down):
    slots = S * TOPK
    flat_ids = expert_ids.reshape(slots).astype(jnp.int32)
    flat_token = jnp.arange(slots, dtype=jnp.int32) // TOPK
    mixing = (gate_scores / lax.optimization_barrier(jnp.sum(gate_scores, axis=1, keepdims=True))).reshape(slots)
    order = jnp.argsort(flat_ids, stable=True).astype(jnp.int32)
    sorted_token = flat_token[order]
    sorted_weight = mixing[order]
    counts = lax.optimization_barrier(jnp.sum((flat_ids[:, None] == jnp.arange(EXPERTS, dtype=jnp.int32)[None, :]).astype(jnp.int32), axis=0))
    starts = (jnp.cumsum(counts) - counts).astype(jnp.int32)
    most = N_CTX * CAP

    def one_expert(total, inputs):
        gate_mat, up_mat, down_mat, start, count = inputs
        offsets = jnp.arange(most, dtype=jnp.int32)
        index = jnp.minimum(start + offsets, slots - 1).astype(jnp.int32)
        live = offsets < count
        row_token = sorted_token[index]
        rows = normed[row_token]
        gate = jnp.dot(rows, gate_mat, preferred_element_type=jnp.float32)
        upper = jnp.dot(rows, up_mat, preferred_element_type=jnp.float32)
        hidden = (jax.nn.silu(gate) * upper).astype(jnp.bfloat16)
        part = jnp.dot(hidden, down_mat, preferred_element_type=jnp.float32).astype(jnp.bfloat16)
        factor = jnp.where(live, sorted_weight[index], jnp.zeros_like(sorted_weight[index]))
        contrib = part.astype(jnp.float32) * factor[:, None]
        return (total.at[row_token].add(contrib), None)
    start_total = jnp.zeros((S, D), jnp.float32)
    total, _ = lax.scan(one_expert, start_total, (w_gate, w_up, w_down, starts, counts))
    return total

def reference(queries, key_rows, value_rows, hidden_in, out_proj, norm_gain, expert_ids, gate_scores, w_gate, w_up, w_down):
    attended = attention(queries, key_rows, value_rows)
    resid = hidden_in.astype(jnp.float32) + jnp.dot(attended, out_proj, preferred_element_type=jnp.float32)
    inverse = lax.rsqrt(lax.optimization_barrier(jnp.mean(resid * resid, axis=1, keepdims=True)) + 1e-06)
    normed = (resid * inverse * norm_gain.astype(jnp.float32)[None, :]).astype(jnp.bfloat16)
    expert_sum = experts_out(normed, expert_ids, gate_scores, w_gate, w_up, w_down)
    return (resid + expert_sum).astype(jnp.bfloat16)
```

```python
import functools
import math

import jax
import jax.numpy as jnp
from jax import lax
from jax.experimental import pallas as pl
from jax.experimental.pallas import tpu as pltpu
from jax.sharding import PartitionSpec as P


HEAD = 128
LOG2E = 1.4426950408889634
HIDE = -1e30
ROOM = 20 << 20


def whole(memory_space=pltpu.VMEM):
    return pl.BlockSpec(memory_space=memory_space)


def cost(flops, size, exps=0):
    return pl.CostEstimate(flops=int(flops), bytes_accessed=int(size), transcendentals=int(exps))


def pack_kernel(key_ref, value_ref, ids_ref, score_ref, rows_ref, mixed_ref):
    count = key_ref.shape[0]
    experts = mixed_ref.shape[0] - count
    both = jnp.concatenate([key_ref[...], value_ref[...]], axis=1)
    rows_ref[...] = both
    mixed_ref[:count, :] = both
    scores = score_ref[...]
    mix = scores / jnp.sum(scores, axis=0, keepdims=True)
    ids = ids_ref[...]
    number = lax.broadcasted_iota(jnp.int32, (experts, count), 0)
    turned = jnp.zeros((experts, count), jnp.float32)
    for k in range(ids.shape[0]):
        turned = turned + jnp.where(number == ids[k : k + 1, :], mix[k : k + 1, :], 0.0)
    high = turned.astype(jnp.bfloat16)
    low = (turned - high.astype(jnp.float32)).astype(jnp.bfloat16)
    mixed_ref[count:, :] = jnp.concatenate([high, low], axis=1)


def pack(key_rows, value_rows, expert_ids, gate_scores, experts):
    count, width = key_rows.shape
    return pl.pallas_call(
        pack_kernel,
        out_shape=(
            jax.ShapeDtypeStruct((count, 2 * width), jnp.bfloat16),
            jax.ShapeDtypeStruct((count + experts, 2 * width), jnp.bfloat16),
        ),
        in_specs=[whole()] * 4,
        out_specs=(whole(), whole()),
        cost_estimate=cost(1e5, 3e5),
        compiler_params=pltpu.CompilerParams(vmem_limit_bytes=ROOM),
        name="pack",
    )(key_rows, value_rows, expert_ids.T, gate_scores.T)


def join_kernel(count, *refs):
    out_ref = refs[-1]
    tail = None
    for n, ref in enumerate(refs[:-1]):
        out_ref[n * count : (n + 1) * count, :] = ref[:count, :]
        if ref.shape[0] > count:
            tail = ref
    out_ref[(len(refs) - 1) * count :, :] = tail[count:, :]


def join(parts, count):
    total = sum(part.shape[0] for part in parts)
    return pl.pallas_call(
        functools.partial(join_kernel, count),
        out_shape=jax.ShapeDtypeStruct((total, parts[0].shape[1]), parts[0].dtype),
        in_specs=[whole()] * len(parts),
        out_specs=whole(),
        cost_estimate=cost(1e5, 4e5),
        compiler_params=pltpu.CompilerParams(vmem_limit_bytes=ROOM),
        name="join",
    )(*parts)


def soften(query, key_ref, value_ref, biases, state):
    scale = HEAD ** (-0.5) * LOG2E
    scores = lax.dot_general(
        query, key_ref[...], (((1,), (1,)), ((), ())), preferred_element_type=jnp.float32
    )
    pieces = [
        scores[:, n * HEAD : (n + 1) * HEAD] + bias for n, bias in enumerate(biases)
    ]
    peak = functools.reduce(jnp.maximum, pieces)
    peak = jnp.max(peak, axis=1, keepdims=True)
    if state is not None:
        peak = jnp.maximum(peak, state[0][:, :1])
    shift = peak * scale
    weights = [jnp.exp2(piece * scale - shift) for piece in pieces]
    total = functools.reduce(jnp.add, weights)
    product = jnp.dot(
        jnp.concatenate([w.astype(jnp.bfloat16) for w in weights], axis=1),
        value_ref[...],
        preferred_element_type=jnp.float32,
    )
    if state is not None:
        factor = jnp.exp2(state[0][:, :1] * scale - shift)
        total = total + state[1] * factor
        product = product + state[2] * factor
    return peak, total, product


def near_kernel(plane, place_ref, query_ref, *refs):
    count = query_ref.shape[0]
    steps = len(refs) - 5
    sources = refs[:steps]
    peak_ref, total_ref, sum_ref, keys, values = refs[steps:]
    for n, ref in enumerate(sources):
        keys[n * count : (n + 1) * count, :] = ref[:count, :HEAD]
        values[n * count : (n + 1) * count, :] = ref[:count, HEAD:]
    me = place_ref[0]
    row = lax.broadcasted_iota(jnp.int32, (count, count), 0)
    column = lax.broadcasted_iota(jnp.int32, (count, count), 1)
    biases = [jnp.where(column <= row, 0.0, HIDE)]
    for step in range(1, plane):
        biases.append(jnp.where((me ^ step) < me, 0.0, HIDE))
    for step in range(1, steps - plane + 1):
        biases.append(jnp.where(me >= step * plane, 0.0, HIDE))
    for head in range(query_ref.shape[1] // HEAD):
        part = slice(head * HEAD, (head + 1) * HEAD)
        peak, total, product = soften(query_ref[:, part], keys, values, biases, None)
        peak_ref[:, part] = jnp.broadcast_to(peak, (count, HEAD))
        total_ref[:, part] = total
        sum_ref[:, part] = product


def near(place, queries, sources, plane):
    count, width = queries.shape
    shape = jax.ShapeDtypeStruct((count, width), jnp.float32)
    keys = len(sources) * count
    return pl.pallas_call(
        functools.partial(near_kernel, plane),
        out_shape=(shape,) * 3,
        in_specs=[whole(pltpu.SMEM)] + [whole()] * (1 + len(sources)),
        out_specs=(whole(),) * 3,
        scratch_shapes=[pltpu.VMEM((keys, HEAD), jnp.bfloat16)] * 2,
        cost_estimate=cost(4 * width * count * keys, 4e6, width * keys),
        compiler_params=pltpu.CompilerParams(vmem_limit_bytes=ROOM),
        name="near",
    )(place, queries, *sources)


def far_kernel(plane, place_ref, query_ref, peak_ref, total_ref, sum_ref, *refs):
    steps = plane - 1
    sources = refs[:steps]
    weight_ref, own_ref, other_ref, keys, values, attended, weight, result, sem = refs[steps:]
    fetch = pltpu.make_async_copy(weight_ref, weight, sem)
    fetch.start()
    count = query_ref.shape[0]
    layers = sources[0].shape[0] // count
    span = layers * count
    for n, ref in enumerate(sources):
        keys[n * span : (n + 1) * span, :] = ref[:span, :HEAD]
        values[n * span : (n + 1) * span, :] = ref[:span, HEAD:]
    me, core = place_ref[0], place_ref[1]
    biases = [jnp.where(me >= step * plane, 0.0, HIDE) for step in range(1, layers + 1)] * steps
    for head in range(query_ref.shape[1] // HEAD):
        part = slice(head * HEAD, (head + 1) * HEAD)
        state = (peak_ref[:, part], total_ref[:, part], sum_ref[:, part])
        _, total, product = soften(query_ref[:, part], keys, values, biases, state)
        denom = jnp.sum(total, axis=1, keepdims=True)
        attended[:, part] = (product / denom).astype(jnp.bfloat16)
    fetch.wait()
    result[...] = jnp.dot(attended[...], weight[...], preferred_element_type=jnp.float32)
    half = count // 2
    own_ref[...] = result[pl.ds(pl.multiple_of(core * half, half), half), :]
    other = result[pl.ds(pl.multiple_of((1 - core) * half, half), half), :]
    other_ref[...] = other.astype(jnp.bfloat16)


def far(place, queries, state, sources, out_proj, plane):
    count, width = queries.shape
    model = out_proj.shape[1]
    keys = len(sources) * (sources[0].shape[0] // count) * count
    return pl.pallas_call(
        functools.partial(far_kernel, plane),
        out_shape=(
            jax.ShapeDtypeStruct((count // 2, model), jnp.float32),
            jax.ShapeDtypeStruct((count // 2, model), jnp.bfloat16),
        ),
        in_specs=[whole(pltpu.SMEM)] + [whole()] * (4 + len(sources)) + [whole(pl.ANY)],
        out_specs=(whole(),) * 2,
        scratch_shapes=[
            pltpu.VMEM((keys, HEAD), jnp.bfloat16),
            pltpu.VMEM((keys, HEAD), jnp.bfloat16),
            pltpu.VMEM((count, width), jnp.bfloat16),
            pltpu.VMEM(out_proj.shape, jnp.bfloat16),
            pltpu.VMEM((count, model), jnp.float32),
            pltpu.SemaphoreType.DMA,
        ],
        cost_estimate=cost(
            4 * width * count * keys + 2 * count * width * model, 6e6, width * keys
        ),
        compiler_params=pltpu.CompilerParams(vmem_limit_bytes=ROOM),
        name="far",
    )(place, queries, *state, *sources, out_proj)


def norm_kernel(place_ref, hidden_ref, own_ref, other_ref, gain_ref, resid_ref, normed_ref):
    half = own_ref.shape[0]
    start = pl.multiple_of(place_ref[1] * half, half)
    hidden = hidden_ref[pl.ds(start, half), :].astype(jnp.float32)
    resid = hidden + own_ref[...] + other_ref[...].astype(jnp.float32)
    inverse = lax.rsqrt(jnp.mean(resid * resid, axis=1, keepdims=True) + 1e-06)
    resid_ref[...] = resid
    normed_ref[...] = (resid * inverse * gain_ref[...]).astype(jnp.bfloat16)


def norm(place, hidden_in, own, other, norm_gain):
    return pl.pallas_call(
        norm_kernel,
        out_shape=(
            jax.ShapeDtypeStruct(own.shape, jnp.float32),
            jax.ShapeDtypeStruct(own.shape, jnp.bfloat16),
        ),
        in_specs=[whole(pltpu.SMEM)] + [whole()] * 4,
        out_specs=(whole(),) * 2,
        cost_estimate=cost(1e6, 1e6),
        compiler_params=pltpu.CompilerParams(vmem_limit_bytes=ROOM),
        name="norm",
    )(place, hidden_in, own, other, norm_gain)


def share_kernel(place_ref, *refs):
    pieces, out_ref, turned = refs[:-2], refs[-2], refs[-1]
    experts, count = pieces[0].shape[0], pieces[0].shape[1] // 2
    half = count // 2
    start = pl.multiple_of(place_ref[1] * half, half)
    number = lax.broadcasted_iota(jnp.int32, (experts, count), 0)
    lane = lax.broadcasted_iota(jnp.int32, (count, count), 1)
    diagonal = lax.broadcasted_iota(jnp.int32, (count, count), 0) == lane
    for n, piece in enumerate(pieces):
        mix = piece[:, :count].astype(jnp.float32) + piece[:, count:].astype(jnp.float32)
        columns = jnp.zeros((count, count), jnp.float32)
        for side in range(2):
            line = jnp.sum(
                jnp.where(number == place_ref[2 + side], mix, 0.0), axis=0, keepdims=True
            )
            column = jnp.sum(jnp.where(diagonal, line, 0.0), axis=1, keepdims=True)
            columns = jnp.where(lane == side, column, columns)
        turned[...] = columns
        out_ref[n * half : (n + 1) * half, :] = turned[pl.ds(start, half), :]


def share(place, pieces, experts):
    width = pieces[0].shape[1]
    count = width // 2
    specs = []
    for piece in pieces:
        block = piece.shape[0] // experts - 1
        specs.append(pl.BlockSpec((experts, width), lambda i, block=block: (block, 0)))
    rows = len(pieces) * count // 2
    return pl.pallas_call(
        share_kernel,
        grid=(1,),
        out_shape=jax.ShapeDtypeStruct((rows, count), jnp.float32),
        in_specs=[whole(pltpu.SMEM)] + specs,
        out_specs=pl.BlockSpec((rows, count), lambda i: (0, 0)),
        scratch_shapes=[pltpu.VMEM((count, count), jnp.float32)],
        cost_estimate=cost(1e6, 4e5),
        compiler_params=pltpu.CompilerParams(vmem_limit_bytes=ROOM),
        name="share",
    )(place, *pieces)


def expert_kernel(first, blocks, place_ref, share_ref, *refs):
    inputs, refs = refs[:blocks], refs[blocks:]
    sources = refs[:9]
    outputs, rows, mats, sems = refs[-8 - blocks : -8], refs[-8], refs[-7:-1], refs[-1]
    core = place_ref[1]
    copies = [pltpu.make_async_copy(sources[n].at[0], mats[n], sems.at[n]) for n in range(3)]
    for n in range(3):
        half = mats[3 + n].shape[0] // 2
        for side in range(2):
            place = core if side == 0 else 1 - core
            target = mats[3 + n].at[pl.ds(pl.multiple_of(place * half, half), half)]
            order = 3 + 2 * n + side
            copies.append(pltpu.make_async_copy(sources[order], target, sems.at[order]))
    for copy in copies:
        copy.start()
    size = inputs[0].shape[0]
    for n, ref in enumerate(inputs):
        rows[n * size : (n + 1) * size, :] = ref[...]
    total = None
    for side in range(2):
        gate_ref, up_ref, down_ref = mats[3 * side : 3 * side + 3]
        waits = [copies[:1], copies[1:2], copies[2:3]] if side == 0 else [
            copies[3:5], copies[5:7], copies[7:9]]
        for copy in waits[0]:
            copy.wait()
        gate = jnp.dot(rows[...], gate_ref[...], preferred_element_type=jnp.float32)
        for copy in waits[1]:
            copy.wait()
        upper = jnp.dot(rows[...], up_ref[...], preferred_element_type=jnp.float32)
        hidden = (gate / (1.0 + jnp.exp(-gate)) * upper).astype(jnp.bfloat16)
        for copy in waits[2]:
            copy.wait()
        part = jnp.dot(hidden, down_ref[...], preferred_element_type=jnp.float32)
        part = part.astype(jnp.bfloat16).astype(jnp.float32)
        factor = share_ref[first * size : (first + blocks) * size, side : side + 1]
        total = part * factor if total is None else total + part * factor
    for n, ref in enumerate(outputs):
        ref[...] = total[n * size : (n + 1) * size, :].astype(ref.dtype)


def experts_on(place, shares, inputs, weights, first, dtypes, after):
    blocks = len(inputs)
    size, model = inputs[0].shape
    units = weights[0].shape[2]
    return pl.pallas_call(
        functools.partial(expert_kernel, first, blocks),
        out_shape=tuple(jax.ShapeDtypeStruct((size, model), dtype) for dtype in dtypes),
        in_specs=[whole(pltpu.SMEM)] + [whole()] * (1 + blocks) + [whole(pl.ANY)] * (9 + len(after)),
        out_specs=tuple([whole()] * blocks),
        scratch_shapes=[pltpu.VMEM((blocks * size, model), jnp.bfloat16)]
        + [
            pltpu.VMEM((model, units), jnp.bfloat16),
            pltpu.VMEM((model, units), jnp.bfloat16),
            pltpu.VMEM((units, model), jnp.bfloat16),
        ]
        * 2
        + [pltpu.SemaphoreType.DMA((9,))],
        cost_estimate=cost(12 * blocks * size * model * units, 12 * model * units),
        compiler_params=pltpu.CompilerParams(vmem_limit_bytes=ROOM),
    )(place, shares, *inputs, *weights, *after)


def final_kernel(place_ref, resid_ref, own_ref, *refs):
    keep_ref, send_ref, work = refs[-3:]
    total = own_ref[...]
    for ref in refs[:-3]:
        total = total + ref[...].astype(jnp.float32)
    work[...] = (resid_ref[...] + total).astype(jnp.bfloat16)
    half = keep_ref.shape[1]
    core = place_ref[1]
    keep_ref[...] = work[:, pl.ds(pl.multiple_of(core * half, half), half)]
    send_ref[...] = work[:, pl.ds(pl.multiple_of((1 - core) * half, half), half)]


def final(place, resid, own, received):
    rows, model = resid.shape
    shape = jax.ShapeDtypeStruct((rows, model // 2), jnp.bfloat16)
    return pl.pallas_call(
        final_kernel,
        out_shape=(shape, shape),
        in_specs=[whole(pltpu.SMEM)] + [whole()] * (2 + len(received)),
        out_specs=(whole(),) * 2,
        scratch_shapes=[pltpu.VMEM((rows, model), jnp.bfloat16)],
        cost_estimate=cost(1e6, 1e6),
        compiler_params=pltpu.CompilerParams(vmem_limit_bytes=ROOM),
        name="final",
    )(place, resid, own, *received)


def compact(
    queries,
    key_rows,
    value_rows,
    hidden_in,
    out_proj,
    norm_gain,
    expert_ids,
    gate_scores,
    w_gate,
    w_up,
    w_down,
):
    count = queries.shape[0]
    model = hidden_in.shape[1]
    ctx = lax.axis_size("ctx")
    plane = math.isqrt(ctx)
    planes = ctx // plane
    away = 2 * plane
    me = lax.axis_index("ctx")
    core = lax.axis_index("exp")
    place = jnp.stack([me, core, me, me ^ plane]).astype(jnp.int32)

    def flip(value, mask):
        return lax.ppermute(value, "ctx", [(i, i ^ mask) for i in range(ctx)])

    def upward(value, step):
        return lax.ppermute(value, "ctx", [(i, i + step) for i in range(ctx - step)])

    def across(value):
        return lax.ppermute(value, "exp", [(0, 1), (1, 0)])

    mates = range(1, plane)
    rows, mixed = pack(key_rows, value_rows, expert_ids, gate_scores, w_gate.shape[0] * ctx)
    column = [
        flip(mixed, away)
        if step == 2
        else upward(rows, step * plane)
        for step in range(1, planes)
    ]
    level = [flip(mixed, mate) for mate in mates]
    joined = join(column, count)
    corner = [flip(joined, mate) for mate in mates]

    halves = []
    for mat in (w_gate, w_up, w_down):
        half = mat.shape[1] // 2
        piece = lax.dynamic_slice_in_dim(mat[0], core * half, half, 0)
        halves.append(flip(piece, plane))
    weights = [w_gate, w_up, w_down]
    for half in halves:
        weights += [half, across(half)]

    state = near(place, queries, [mixed] + level + column, plane)
    own, other = far(place, queries, state, corner, out_proj, plane)
    resid, normed = norm(place, hidden_in, own, across(other), norm_gain.reshape(1, model))

    shares = share(place, [mixed] + level + [column[1]] + corner, w_gate.shape[0] * ctx)
    opposite = flip(normed, away)
    level_rows = [flip(normed, mate) for mate in mates]
    corner_rows = [flip(opposite, mate) for mate in mates]
    f32, bf16 = jnp.float32, jnp.bfloat16
    near_out = experts_on(
        place, shares, [normed] + level_rows + [opposite], weights, 0,
        [f32] + [bf16] * len(mates) + [f32], [],
    )
    far_out = experts_on(
        place, shares, corner_rows, weights, plane + 1, [bf16] * len(mates),
        [near_out[1]],
    )
    passed = [flip(value, mate) for value, mate in zip(far_out, mates)]
    direct = [flip(value, mate) for value, mate in zip(near_out[1:plane], mates)]
    last = flip(gather_sum(near_out[plane], passed), away)
    keep, send = final(place, resid, near_out[0], direct + [last])
    return assemble(place, keep, across(send))


def gather_sum_kernel(own_ref, *refs):
    total = own_ref[...]
    for ref in refs[:-1]:
        total = total + ref[...].astype(jnp.float32)
    refs[-1][...] = total.astype(jnp.bfloat16)


def gather_sum(own, received):
    return pl.pallas_call(
        gather_sum_kernel,
        out_shape=jax.ShapeDtypeStruct(own.shape, jnp.bfloat16),
        in_specs=[whole()] * (1 + len(received)),
        out_specs=whole(),
        cost_estimate=cost(1e5, 8e5),
        compiler_params=pltpu.CompilerParams(vmem_limit_bytes=ROOM),
        name="gather_sum",
    )(own, *received)


def assemble_kernel(place_ref, keep_ref, received_ref, out_ref):
    half = keep_ref.shape[0]
    core = place_ref[1]
    out_ref[pl.ds(pl.multiple_of(core * half, half), half), :] = keep_ref[...]
    out_ref[pl.ds(pl.multiple_of((1 - core) * half, half), half), :] = received_ref[...]


def assemble(place, keep, received):
    return pl.pallas_call(
        assemble_kernel,
        out_shape=jax.ShapeDtypeStruct((2 * keep.shape[0], keep.shape[1]), keep.dtype),
        in_specs=[whole(pltpu.SMEM)] + [whole()] * 2,
        out_specs=whole(),
        cost_estimate=cost(1e5, 3e5),
        compiler_params=pltpu.CompilerParams(vmem_limit_bytes=ROOM),
        name="assemble",
    )(place, keep, received)


def fits_compact(queries, key_rows, expert_ids, w_gate):
    ctx = lax.axis_size("ctx")
    plane = math.isqrt(ctx)
    return (
        plane * plane == ctx
        and plane == 4
        and lax.axis_size("exp") == 2
        and w_gate.shape[0] == 1
        and ctx <= 2 * expert_ids.shape[1]
        and key_rows.shape == (HEAD, HEAD)
        and queries.shape[0] == HEAD
    )


def attend(queries, key_rows, value_rows, first):
    token_count = queries.shape[0]
    kv_heads = key_rows.shape[1] // 128
    q_heads = queries.shape[1] // 128
    group = q_heads // kv_heads
    grouped = queries.reshape(token_count, kv_heads, group, 128)
    query_pos = first + jnp.arange(token_count, dtype=jnp.int32)
    last_pos = first + token_count - 1
    scale = 128 ** (-0.5)
    shape_rows = (kv_heads, group, token_count)
    start_state = (
        jnp.full(shape_rows, -1e30, jnp.float32),
        jnp.zeros(shape_rows, jnp.float32),
        jnp.zeros(shape_rows + (128,), jnp.float32),
    )
    key_piece = lax.all_gather(key_rows, "ctx", axis=0, tiled=True)
    value_piece = lax.all_gather(value_rows, "ctx", axis=0, tiled=True)
    count = key_piece.shape[0]
    width = math.gcd(count, 512)

    def step(block_index, state):
        offset = block_index * width

        def compute(inner):
            running_max, running_sum, accum = inner
            key_block = lax.dynamic_slice_in_dim(key_piece, block_index * width, width, 0).reshape(
                width, kv_heads, 128
            )
            value_block = lax.dynamic_slice_in_dim(
                value_piece, block_index * width, width, 0
            ).reshape(width, kv_heads, 128)
            scores = (
                jnp.einsum("tkgd,skd->kgts", grouped, key_block, preferred_element_type=jnp.float32)
                * scale
            )
            key_pos = offset + jnp.arange(width, dtype=jnp.int32)
            allowed = key_pos[None, :] <= query_pos[:, None]
            scores = jnp.where(allowed, scores, -jnp.inf)
            new_max = jnp.maximum(running_max, jnp.max(scores, axis=-1))
            factor = jnp.exp(running_max - new_max)
            weights = jnp.exp(scores - new_max[..., None])
            new_sum = running_sum * factor + jnp.sum(weights, axis=-1)
            product = jnp.einsum(
                "kgts,skd->kgtd",
                weights.astype(jnp.bfloat16),
                value_block,
                preferred_element_type=jnp.float32,
            )
            return (new_max, new_sum, accum * factor[..., None] + product)

        return lax.cond(offset <= last_pos, compute, lambda inner: inner, state)

    _, total, accum = lax.fori_loop(0, count // width, step, start_state)
    output = accum / total[..., None]
    return (
        jnp.transpose(output, (2, 0, 1, 3)).reshape(token_count, q_heads * 128).astype(jnp.bfloat16)
    )


def place_rows(expert_ids, sent_rows, capacity, expert_count):
    top_count = expert_ids.shape[1]
    flat_ids = expert_ids.reshape(-1)
    onehot = (flat_ids[:, None] == jnp.arange(expert_count, dtype=jnp.int32)[None, :]).astype(
        jnp.int32
    )
    earlier = jnp.cumsum(onehot, axis=0) - onehot
    slot_index = jnp.sum(earlier * onehot, axis=1)
    destination = flat_ids * capacity + slot_index
    copies = jnp.repeat(sent_rows, top_count, axis=0)
    buffer = (
        jnp.zeros((expert_count * capacity, sent_rows.shape[1]), sent_rows.dtype)
        .at[destination]
        .set(copies)
    )
    return (buffer.reshape(expert_count, 2, capacity // 2, sent_rows.shape[1]), destination)


def per_device(
    queries,
    key_rows,
    value_rows,
    hidden_in,
    out_proj,
    norm_gain,
    expert_ids,
    gate_scores,
    w_gate,
    w_up,
    w_down,
):
    if fits_compact(queries, key_rows, expert_ids, w_gate):
        return compact(
            queries, key_rows, value_rows, hidden_in, out_proj, norm_gain,
            expert_ids, gate_scores, w_gate, w_up, w_down,
        )
    token_count = queries.shape[0]
    model_width = hidden_in.shape[1]
    half_width = model_width // 2
    ctx_size = lax.axis_size("ctx")
    local_experts = w_gate.shape[0]
    expert_count = local_experts * ctx_size
    top_count = expert_ids.shape[1]
    capacity = 2 * (
        min(token_count, max(2, 3 * token_count * top_count // (2 * expert_count))) // 2
    )
    half_cap = capacity // 2
    first = lax.axis_index("ctx") * token_count
    core = lax.axis_index("exp")
    side_start = core * half_width
    attended = attend(queries, key_rows, value_rows, first)
    head_part = jnp.dot(attended, out_proj, preferred_element_type=jnp.float32)
    attn_full = lax.psum(head_part.astype(jnp.bfloat16), "exp").astype(jnp.float32)
    resid = hidden_in.astype(jnp.float32) + attn_full
    inverse = lax.rsqrt(jnp.mean(resid * resid, axis=1, keepdims=True) + 1e-06)
    sent_rows = (resid * inverse * norm_gain[None, :]).astype(jnp.bfloat16)
    resid_half = lax.dynamic_slice_in_dim(resid, side_start, half_width, 1)
    buffer, destination = place_rows(expert_ids, sent_rows, capacity, expert_count)
    own_slots = lax.dynamic_slice_in_dim(buffer, core, 1, 1)
    grouped = lax.all_to_all(own_slots, "ctx", split_axis=0, concat_axis=0, tiled=True)
    gate = jnp.einsum("sxmd,xdf->sxmf", grouped, w_gate, preferred_element_type=jnp.float32)
    upper = jnp.einsum("sxmd,xdf->sxmf", grouped, w_up, preferred_element_type=jnp.float32)
    hidden = (jax.nn.silu(gate) * upper).astype(jnp.bfloat16)
    partial_value = jnp.einsum(
        "sxmf,xfd->sxmd", hidden, w_down, preferred_element_type=jnp.float32
    ).astype(jnp.bfloat16)
    returned = lax.all_to_all(partial_value, "ctx", split_axis=0, concat_axis=0, tiled=True)
    flat_back = returned.reshape(expert_count * half_cap, model_width)
    slot_of = destination % capacity
    expert_of = destination // capacity
    owned = slot_of // half_cap == core
    local_index = jnp.where(owned, expert_of * half_cap + slot_of - core * half_cap, 0)
    picked = flat_back[local_index].astype(jnp.float32)
    mixing = (gate_scores / jnp.sum(gate_scores, axis=1, keepdims=True)).reshape(-1)
    mixing = jnp.where(owned, mixing, 0.0)
    weighted = (picked * mixing[:, None]).reshape(token_count, top_count, model_width)
    mixed_part = jnp.sum(weighted, axis=1)
    moe_half = lax.psum_scatter(
        mixed_part.astype(jnp.bfloat16), "exp", scatter_dimension=1, tiled=True
    ).astype(jnp.float32)
    return (resid_half + moe_half).astype(jnp.bfloat16)


def solution(mesh):
    placed = (
        P(("groups", "ctx"), "exp"),
        P(("groups", "ctx"), "exp"),
        P(("groups", "ctx"), "exp"),
        P(("groups", "ctx"), None),
        P("exp", None),
        P(),
        P(("groups", "ctx"), None),
        P(("groups", "ctx"), None),
        P("ctx", None, None),
        P("ctx", None, None),
        P("ctx", None, None),
    )
    return jax.shard_map(
        per_device,
        mesh=mesh,
        in_specs=placed,
        out_specs=P(("groups", "ctx"), "exp"),
        check_vma=False,
    )
```

```python
import functools
import math

import jax
import jax.numpy as jnp
from jax import lax
from jax.experimental import pallas as pl
from jax.experimental.pallas import tpu as pltpu
from jax.sharding import PartitionSpec as P


HEAD = 128
LOG2E = 1.4426950408889634
HIDE = -1e30
ROOM = 20 << 20
GROUP = 512
FULL = 62 << 20


def whole(memory_space=pltpu.VMEM):
    return pl.BlockSpec(memory_space=memory_space)


def cost(flops, size, exps=0):
    return pl.CostEstimate(flops=int(flops), bytes_accessed=int(size), transcendentals=int(exps))


def fetch_all(pairs, sems):
    copies = [
        pltpu.make_async_copy(source, target, sems.at[n])
        for n, (source, target) in enumerate(pairs)
    ]
    for copy in copies:
        copy.start()
    return copies


def pack_kernel(key_ref, value_ref, ids_ref, score_ref, rows_ref, mixed_ref, both, ids, score, sems):
    count, width = key_ref.shape
    copies = fetch_all(
        [
            (key_ref, both.at[:, :width]),
            (value_ref, both.at[:, width:]),
            (ids_ref, ids),
            (score_ref, score),
        ],
        sems,
    )
    for copy in copies:
        copy.wait()
    rows_ref[...] = both[...]
    mixed_ref[:count, :] = both[...]
    experts = mixed_ref.shape[0] - count
    mix = score[...] / jnp.sum(score[...], axis=0, keepdims=True)
    number = lax.broadcasted_iota(jnp.int32, (experts, count), 0)
    turned = jnp.zeros((experts, count), jnp.float32)
    for k in range(ids.shape[0]):
        turned = turned + jnp.where(number == ids[k : k + 1, :], mix[k : k + 1, :], 0.0)
    high = turned.astype(jnp.bfloat16)
    low = (turned - high.astype(jnp.float32)).astype(jnp.bfloat16)
    mixed_ref[count:, :] = jnp.concatenate([high, low], axis=1)


def pack(key_rows, value_rows, expert_ids, gate_scores, experts):
    count, width = key_rows.shape
    top = expert_ids.shape[1]
    return pl.pallas_call(
        pack_kernel,
        out_shape=(
            jax.ShapeDtypeStruct((count, 2 * width), jnp.bfloat16),
            jax.ShapeDtypeStruct((count + experts, 2 * width), jnp.bfloat16),
        ),
        in_specs=[whole(pltpu.HBM)] * 4,
        out_specs=(whole(), whole()),
        scratch_shapes=[
            pltpu.VMEM((count, 2 * width), jnp.bfloat16),
            pltpu.VMEM((top, count), jnp.int32),
            pltpu.VMEM((top, count), jnp.float32),
            pltpu.SemaphoreType.DMA((4,)),
        ],
        cost_estimate=cost(1e5, 3e5),
        compiler_params=pltpu.CompilerParams(vmem_limit_bytes=FULL),
        name="pack",
    )(key_rows, value_rows, expert_ids.T, gate_scores.T)


def stack_kernel(place_ref, gate_ref, up_ref, mine_ref, other_ref, own_wide, swapped_wide, sems):
    units, core = gate_ref.shape[2], place_ref[1]
    mine = pl.ds(pl.multiple_of(core * units, units), units)
    other = pl.ds(pl.multiple_of((1 - core) * units, units), units)
    pairs = [
        (gate_ref.at[0], own_wide.at[:, :units]),
        (up_ref.at[0], own_wide.at[:, units:]),
        (mine_ref, swapped_wide.at[:, mine]),
        (other_ref, swapped_wide.at[:, other]),
    ]
    for copy in fetch_all(pairs, sems):
        copy.wait()


def stack(place, w_gate, w_up, mine, other):
    _, model, units = w_gate.shape
    return pl.pallas_call(
        stack_kernel,
        out_shape=(jax.ShapeDtypeStruct((model, 2 * units), jnp.bfloat16),) * 2,
        in_specs=[whole(pltpu.SMEM)] + [whole(pl.ANY)] * 4,
        out_specs=(whole(),) * 2,
        scratch_shapes=[pltpu.SemaphoreType.DMA((4,))],
        cost_estimate=cost(1e5, 6e6),
        compiler_params=pltpu.CompilerParams(vmem_limit_bytes=ROOM),
        name="stack",
    )(place, w_gate, w_up, mine, other)


def join_kernel(count, *refs):
    out_ref = refs[-1]
    tail = None
    for n, ref in enumerate(refs[:-1]):
        out_ref[n * count : (n + 1) * count, :] = ref[:count, :]
        if ref.shape[0] > count:
            tail = ref
    out_ref[(len(refs) - 1) * count :, :] = tail[count:, :]


def join(parts, count):
    total = sum(part.shape[0] for part in parts)
    return pl.pallas_call(
        functools.partial(join_kernel, count),
        out_shape=jax.ShapeDtypeStruct((total, parts[0].shape[1]), parts[0].dtype),
        in_specs=[whole()] * len(parts),
        out_specs=whole(),
        cost_estimate=cost(1e5, 4e5),
        compiler_params=pltpu.CompilerParams(vmem_limit_bytes=ROOM),
        name="join",
    )(*parts)


def soften(query, keys, values, biases, state):
    scale = HEAD ** (-0.5) * LOG2E
    scores = lax.dot_general(
        query, keys, (((1,), (1,)), ((), ())), preferred_element_type=jnp.float32
    )
    pieces = [scores[:, n * HEAD : (n + 1) * HEAD] for n in range(keys.shape[0] // HEAD)]
    if biases is not None:
        pieces = [piece + bias for piece, bias in zip(pieces, biases)]
    peak = functools.reduce(jnp.maximum, pieces)
    peak = jnp.max(peak, axis=1, keepdims=True)
    if state is not None:
        peak = jnp.maximum(peak, state[0][:, :1])
    shift = peak * scale
    weights = [jnp.exp2(piece * scale - shift) for piece in pieces]
    total = functools.reduce(jnp.add, weights)
    product = jnp.dot(
        jnp.concatenate([w.astype(jnp.bfloat16) for w in weights], axis=1),
        values,
        preferred_element_type=jnp.float32,
    )
    if state is not None:
        factor = jnp.exp2(state[0][:, :1] * scale - shift)
        total = total + state[1] * factor
        product = product + state[2] * factor
    return peak, total, product


def near_kernel(plane, place_ref, query_ref, *refs):
    sources, column_ref = refs[:plane], refs[plane]
    heads_ref, peak_ref, total_ref, sum_ref, keys, values, sems = refs[plane + 1 :]
    count = query_ref.shape[0]
    pairs = []
    for head in range(query_ref.shape[1] // HEAD):
        part = slice(head * count, (head + 1) * count)
        pairs.append((query_ref.at[:, head * HEAD : (head + 1) * HEAD], heads_ref.at[part]))
    copies = fetch_all(pairs, sems)
    layers = column_ref.shape[0] // count
    for n, ref in enumerate(sources):
        keys[n * count : (n + 1) * count, :] = ref[:count, :HEAD]
        values[n * count : (n + 1) * count, :] = ref[:count, HEAD:]
    keys[plane * count :, :] = column_ref[: layers * count, :HEAD]
    values[plane * count :, :] = column_ref[: layers * count, HEAD:]
    me = place_ref[0]
    row = lax.broadcasted_iota(jnp.int32, (GROUP, count), 0) % count
    number = lax.broadcasted_iota(jnp.int32, (GROUP, count), 1)
    biases = [jnp.where(number <= row, 0.0, HIDE)]
    for step in range(1, plane):
        biases.append(jnp.where((me ^ step) < me, 0.0, HIDE))
    for step in range(1, layers + 1):
        biases.append(jnp.where(me >= step * plane, 0.0, HIDE))
    for copy in copies:
        copy.wait()
    for start in range(0, heads_ref.shape[0], GROUP):
        part = slice(start, start + GROUP)
        peak, total, product = soften(heads_ref[part], keys[...], values[...], biases, None)
        peak_ref[part] = jnp.broadcast_to(peak, (GROUP, HEAD))
        total_ref[part] = total
        sum_ref[part] = product


def near(place, queries, sources, column, plane):
    count, width = queries.shape
    rows = count * width // HEAD
    shape = jax.ShapeDtypeStruct((rows, HEAD), jnp.float32)
    keys = (plane + column.shape[0] // HEAD) * HEAD
    return pl.pallas_call(
        functools.partial(near_kernel, plane),
        out_shape=(jax.ShapeDtypeStruct((rows, HEAD), jnp.bfloat16),) + (shape,) * 3,
        in_specs=[whole(pltpu.SMEM), whole(pl.ANY)] + [whole()] * (1 + len(sources)),
        out_specs=(whole(),) * 4,
        scratch_shapes=[pltpu.VMEM((keys, HEAD), jnp.bfloat16)] * 2
        + [pltpu.SemaphoreType.DMA((width // HEAD,))],
        cost_estimate=cost(4 * rows * HEAD * keys, 4e6, rows * keys),
        compiler_params=pltpu.CompilerParams(vmem_limit_bytes=ROOM),
        name="near",
    )(place, queries, *sources, column)


def extend(plane, place_ref, query_ref, state, sources, keys, values, out):
    count = HEAD
    layers = sources[0].shape[0] // count
    height = place_ref[0] // plane

    @pl.when(height == 0)
    def _():
        for source, target in zip(state, out):
            target[...] = source[...]

    for used in range(1, layers + 1):

        @pl.when(height == used)
        def _(used=used):
            span = used * count
            for n, ref in enumerate(sources):
                keys[n * span : (n + 1) * span, :] = ref[:span, :HEAD]
                values[n * span : (n + 1) * span, :] = ref[:span, HEAD:]
            size = len(sources) * span
            for start in range(0, query_ref.shape[0], GROUP):
                part = slice(start, start + GROUP)
                peak, total, product = soften(
                    query_ref[part],
                    keys[:size],
                    values[:size],
                    None,
                    [ref[part] for ref in state],
                )
                out[0][part] = jnp.broadcast_to(peak, (GROUP, HEAD))
                out[1][part] = total
                out[2][part] = product


def more_kernel(plane, steps, place_ref, query_ref, *refs):
    state, sources, refs = refs[:3], refs[3 : 3 + steps], refs[3 + steps :]
    extend(plane, place_ref, query_ref, state, sources, refs[3], refs[4], refs[:3])


def more(place, heads, state, sources, plane):
    shape = jax.ShapeDtypeStruct(heads.shape, jnp.float32)
    keys = len(sources) * (sources[0].shape[0] // HEAD) * HEAD
    return pl.pallas_call(
        functools.partial(more_kernel, plane, len(sources)),
        out_shape=(shape,) * 3,
        in_specs=[whole(pltpu.SMEM)] + [whole()] * (4 + len(sources)),
        out_specs=(whole(),) * 3,
        scratch_shapes=[pltpu.VMEM((keys, HEAD), jnp.bfloat16)] * 2,
        cost_estimate=cost(4 * heads.size * keys, 4e6, heads.shape[0] * keys),
        compiler_params=pltpu.CompilerParams(vmem_limit_bytes=ROOM),
        name="more",
    )(place, heads, *state, *sources)


def far_kernel(plane, place_ref, query_ref, peak_ref, total_ref, sum_ref, source_ref, *refs):
    weight_ref, own_ref, other_ref, keys, values, peak, total, product, attended, result = refs
    state, work = (peak_ref, total_ref, sum_ref), (peak, total, product)
    extend(plane, place_ref, query_ref, state, (source_ref,), keys, values, work)
    count = attended.shape[0]
    core = place_ref[1]
    for head in range(query_ref.shape[0] // count):
        part = slice(head * count, (head + 1) * count)
        denom = jnp.sum(total[part], axis=1, keepdims=True)
        attended[:, head * HEAD : (head + 1) * HEAD] = (product[part] / denom).astype(jnp.bfloat16)
    result[...] = jnp.dot(attended[...], weight_ref[...], preferred_element_type=jnp.float32)
    half = count // 2
    own_ref[...] = result[pl.ds(pl.multiple_of(core * half, half), half), :]
    other = result[pl.ds(pl.multiple_of((1 - core) * half, half), half), :]
    other_ref[...] = other.astype(jnp.bfloat16)


def far(place, heads, state, source, out_proj, plane):
    width, model = out_proj.shape
    count = heads.size // width
    keys = source.shape[0] // HEAD * HEAD
    return pl.pallas_call(
        functools.partial(far_kernel, plane),
        out_shape=(
            jax.ShapeDtypeStruct((count // 2, model), jnp.float32),
            jax.ShapeDtypeStruct((count // 2, model), jnp.bfloat16),
        ),
        in_specs=[whole(pltpu.SMEM)] + [whole()] * 6,
        out_specs=(whole(),) * 2,
        scratch_shapes=[pltpu.VMEM((keys, HEAD), jnp.bfloat16)] * 2
        + [pltpu.VMEM(heads.shape, jnp.float32)] * 3
        + [
            pltpu.VMEM((count, width), jnp.bfloat16),
            pltpu.VMEM((count, model), jnp.float32),
        ],
        cost_estimate=cost(
            4 * heads.size * keys + 2 * count * width * model, 6e6, heads.shape[0] * keys
        ),
        compiler_params=pltpu.CompilerParams(vmem_limit_bytes=ROOM),
        name="far",
    )(place, heads, *state, source, out_proj)


def norm_kernel(place_ref, hidden_ref, own_ref, other_ref, gain_ref, resid_ref, normed_ref):
    half = own_ref.shape[0]
    start = pl.multiple_of(place_ref[1] * half, half)
    hidden = hidden_ref[pl.ds(start, half), :].astype(jnp.float32)
    resid = hidden + own_ref[...] + other_ref[...].astype(jnp.float32)
    inverse = lax.rsqrt(jnp.mean(resid * resid, axis=1, keepdims=True) + 1e-06)
    resid_ref[...] = resid
    normed_ref[...] = (resid * inverse * gain_ref[...]).astype(jnp.bfloat16)


def norm(place, hidden_in, own, other, norm_gain):
    return pl.pallas_call(
        norm_kernel,
        out_shape=(
            jax.ShapeDtypeStruct(own.shape, jnp.float32),
            jax.ShapeDtypeStruct(own.shape, jnp.bfloat16),
        ),
        in_specs=[whole(pltpu.SMEM)] + [whole()] * 4,
        out_specs=(whole(),) * 2,
        cost_estimate=cost(1e6, 1e6),
        compiler_params=pltpu.CompilerParams(vmem_limit_bytes=ROOM),
        name="norm",
    )(place, hidden_in, own, other, norm_gain)


def share_kernel(place_ref, *refs):
    pieces, out_ref, turned = refs[:-2], refs[-2], refs[-1]
    experts, count = pieces[0].shape[0], pieces[0].shape[1] // 2
    half = count // 2
    start = pl.multiple_of(place_ref[1] * half, half)
    number = lax.broadcasted_iota(jnp.int32, (experts, count), 0)
    lane = lax.broadcasted_iota(jnp.int32, (count, count), 1)
    diagonal = lax.broadcasted_iota(jnp.int32, (count, count), 0) == lane
    for n, piece in enumerate(pieces):
        mix = piece[:, :count].astype(jnp.float32) + piece[:, count:].astype(jnp.float32)
        columns = jnp.zeros((count, count), jnp.float32)
        for side in range(2):
            line = jnp.sum(
                jnp.where(number == place_ref[2 + side], mix, 0.0), axis=0, keepdims=True
            )
            column = jnp.sum(jnp.where(diagonal, line, 0.0), axis=1, keepdims=True)
            columns = jnp.where(lane == side, column, columns)
        turned[...] = columns
        out_ref[n * half : (n + 1) * half, :] = turned[pl.ds(start, half), :]


def share(place, pieces, experts):
    width = pieces[0].shape[1]
    count = width // 2
    specs = []
    for piece in pieces:
        block = piece.shape[0] // experts - 1
        specs.append(pl.BlockSpec((experts, width), lambda i, block=block: (block, 0)))
    rows = len(pieces) * count // 2
    return pl.pallas_call(
        share_kernel,
        grid=(1,),
        out_shape=jax.ShapeDtypeStruct((rows, count), jnp.float32),
        in_specs=[whole(pltpu.SMEM)] + specs,
        out_specs=pl.BlockSpec((rows, count), lambda i: (0, 0)),
        scratch_shapes=[pltpu.VMEM((count, count), jnp.float32)],
        cost_estimate=cost(1e6, 4e5),
        compiler_params=pltpu.CompilerParams(vmem_limit_bytes=ROOM),
        name="columns",
    )(place, *pieces)


def expert_rows(share_ref, first, inputs, wide_refs, rows, hidden):
    size = inputs[0].shape[0]
    units = wide_refs[0].shape[1] // 2
    for n, ref in enumerate(inputs):
        rows[n * size : (n + 1) * size, :] = ref[...]
    for side, wide_ref in enumerate(wide_refs):
        both = jnp.dot(rows[...], wide_ref[...], preferred_element_type=jnp.float32)
        gate, upper = both[:, :units], both[:, units:]
        factor = share_ref[first * size : (first + len(inputs)) * size, side : side + 1]
        value = gate / (1.0 + jnp.exp(-gate)) * upper * factor
        hidden[:, side * units : (side + 1) * units] = value.astype(jnp.bfloat16)


def expert_sums(hidden, tall_ref, outputs):
    size = outputs[0].shape[0]
    total = jnp.dot(hidden[...], tall_ref[...], preferred_element_type=jnp.float32)
    for n, ref in enumerate(outputs):
        ref[...] = total[n * size : (n + 1) * size, :].astype(ref.dtype)


def expert_near_kernel(blocks, place_ref, share_ref, *refs):
    inputs, wide_refs, refs = refs[:blocks], refs[blocks : blocks + 2], refs[blocks + 2 :]
    down_ref, pieces = refs[0], refs[1:5]
    outputs, tall_ref, rows, hidden, sems = refs[5 : 5 + blocks], *refs[5 + blocks :]
    units, core = down_ref.shape[1], place_ref[1]
    size = pieces[0].shape[0]
    pairs = [(down_ref.at[0], tall_ref.at[:units])]
    for n, position in enumerate((core, 1 - core)):
        for part, ref in enumerate(pieces[n::2]):
            start = units + position * (units // 2) + part * size
            pairs.append((ref, tall_ref.at[pl.ds(pl.multiple_of(start, size), size)]))
    copies = fetch_all(pairs, sems)
    expert_rows(share_ref, 0, inputs, wide_refs, rows, hidden)
    for copy in copies:
        copy.wait()
    expert_sums(hidden, tall_ref, outputs)


def expert_far_kernel(first, blocks, share_ref, *refs):
    inputs, wide_refs, tall_ref = refs[:blocks], refs[blocks : blocks + 2], refs[blocks + 2]
    outputs, rows, hidden = refs[blocks + 3 : -2], refs[-2], refs[-1]
    expert_rows(share_ref, first, inputs, wide_refs, rows, hidden)
    expert_sums(hidden, tall_ref, outputs)


def experts_near(place, shares, inputs, wide, w_down, pieces, dtypes):
    blocks = len(inputs)
    size, model = inputs[0].shape
    both = 2 * w_down.shape[1]
    return pl.pallas_call(
        functools.partial(expert_near_kernel, blocks),
        out_shape=tuple(jax.ShapeDtypeStruct((size, model), dtype) for dtype in dtypes)
        + (jax.ShapeDtypeStruct((both, model), jnp.bfloat16),),
        in_specs=[whole(pltpu.SMEM)] + [whole()] * (3 + blocks) + [whole(pl.ANY)] * 5,
        out_specs=(whole(),) * (blocks + 1),
        scratch_shapes=[
            pltpu.VMEM((blocks * size, model), jnp.bfloat16),
            pltpu.VMEM((blocks * size, both), jnp.bfloat16),
            pltpu.SemaphoreType.DMA((5,)),
        ],
        cost_estimate=cost(6 * blocks * size * model * both, 6 * model * both),
        compiler_params=pltpu.CompilerParams(vmem_limit_bytes=ROOM),
        name="experts_near",
    )(place, shares, *inputs, *wide, w_down, *pieces)


def experts_far(shares, inputs, wide, tall, first):
    blocks = len(inputs)
    size, model = inputs[0].shape
    both = tall.shape[0]
    return pl.pallas_call(
        functools.partial(expert_far_kernel, first, blocks),
        out_shape=(jax.ShapeDtypeStruct((size, model), jnp.bfloat16),) * blocks,
        in_specs=[whole()] * (4 + blocks),
        out_specs=(whole(),) * blocks,
        scratch_shapes=[
            pltpu.VMEM((blocks * size, model), jnp.bfloat16),
            pltpu.VMEM((blocks * size, both), jnp.bfloat16),
        ],
        cost_estimate=cost(6 * blocks * size * model * both, 6 * model * both),
        compiler_params=pltpu.CompilerParams(vmem_limit_bytes=ROOM),
        name="experts_far",
    )(shares, *inputs, *wide, tall)


def final_kernel(place_ref, resid_ref, own_ref, *refs):
    keep_ref, send_ref, work = refs[-3:]
    total = own_ref[...]
    for ref in refs[:-3]:
        total = total + ref[...].astype(jnp.float32)
    work[...] = (resid_ref[...] + total).astype(jnp.bfloat16)
    half = keep_ref.shape[1]
    core = place_ref[1]
    keep_ref[...] = work[:, pl.ds(pl.multiple_of(core * half, half), half)]
    send_ref[...] = work[:, pl.ds(pl.multiple_of((1 - core) * half, half), half)]


def final(place, resid, own, received):
    rows, model = resid.shape
    shape = jax.ShapeDtypeStruct((rows, model // 2), jnp.bfloat16)
    return pl.pallas_call(
        final_kernel,
        out_shape=(shape, shape),
        in_specs=[whole(pltpu.SMEM)] + [whole()] * (2 + len(received)),
        out_specs=(whole(),) * 2,
        scratch_shapes=[pltpu.VMEM((rows, model), jnp.bfloat16)],
        cost_estimate=cost(1e6, 1e6),
        compiler_params=pltpu.CompilerParams(vmem_limit_bytes=ROOM),
        name="final",
    )(place, resid, own, *received)


def compact(
    queries,
    key_rows,
    value_rows,
    hidden_in,
    out_proj,
    norm_gain,
    expert_ids,
    gate_scores,
    w_gate,
    w_up,
    w_down,
):
    count = queries.shape[0]
    model = hidden_in.shape[1]
    ctx = lax.axis_size("ctx")
    plane = math.isqrt(ctx)
    planes = ctx // plane
    away = 2 * plane
    me = lax.axis_index("ctx")
    core = lax.axis_index("exp")
    place = jnp.stack([me, core, me, me ^ plane]).astype(jnp.int32)

    def flip(value, mask):
        return lax.ppermute(value, "ctx", [(i, i ^ mask) for i in range(ctx)])

    def upward(value, step):
        return lax.ppermute(value, "ctx", [(i, i + step) for i in range(ctx - step)])

    def across(value):
        return lax.ppermute(value, "exp", [(0, 1), (1, 0)])

    mates = range(1, plane)
    rows, mixed = pack(key_rows, value_rows, expert_ids, gate_scores, w_gate.shape[0] * ctx)
    column = [
        flip(mixed, away)
        if step == 2
        else upward(rows, step * plane)
        for step in range(1, planes)
    ]
    level = [flip(mixed, mate) for mate in mates]
    joined = join(column, count)
    corner = [flip(joined, mate) for mate in mates]

    units = w_gate.shape[2]
    quarter = units // 4

    def half_flip(value, side):
        pairs = [(2 * i + side, 2 * (i ^ plane) + side) for i in range(ctx)]
        return lax.ppermute(value, ("ctx", "exp"), pairs)

    gate_swap = half_flip(w_gate[0], 0)
    up_swap = half_flip(w_up[0], 1)
    tall_swap = []
    for part in range(2):
        start = core * 2 * quarter + part * quarter
        piece = lax.dynamic_slice_in_dim(w_down[0], start, quarter, 0)
        tall_swap.append(flip(piece, plane))

    heads, *state = near(place, queries, [mixed] + level, joined, plane)
    state = more(place, heads, state, corner[:-1], plane)
    own, other = far(place, heads, state, corner[-1], out_proj, plane)
    resid, normed = norm(place, hidden_in, own, across(other), norm_gain.reshape(1, model))
    wide_swap = gate_swap + up_swap
    wide = stack(place, w_gate, w_up, wide_swap, across(wide_swap))
    pieces = [value for piece in tall_swap for value in (piece, across(piece))]

    shares = share(place, [mixed] + level + [joined] + corner, w_gate.shape[0] * ctx)
    opposite = flip(normed, away)
    level_rows = [flip(normed, mate) for mate in mates]
    corner_rows = [flip(opposite, mate) for mate in mates]
    f32, bf16 = jnp.float32, jnp.bfloat16
    *near_out, tall = experts_near(
        place, shares, [normed] + level_rows + [opposite], wide, w_down, pieces,
        [f32] + [bf16] * len(mates) + [f32],
    )
    far_out = experts_far(shares, corner_rows, wide, tall, plane + 1)
    passed = [flip(value, mate) for value, mate in zip(far_out, mates)]
    direct = [flip(value, mate) for value, mate in zip(near_out[1:plane], mates)]
    last = flip(gather_sum(near_out[plane], passed), away)
    keep, send = final(place, resid, near_out[0], direct + [last])
    return assemble(place, keep, across(send))


def gather_sum_kernel(own_ref, *refs):
    total = own_ref[...]
    for ref in refs[:-1]:
        total = total + ref[...].astype(jnp.float32)
    refs[-1][...] = total.astype(jnp.bfloat16)


def gather_sum(own, received):
    return pl.pallas_call(
        gather_sum_kernel,
        out_shape=jax.ShapeDtypeStruct(own.shape, jnp.bfloat16),
        in_specs=[whole()] * (1 + len(received)),
        out_specs=whole(),
        cost_estimate=cost(1e5, 8e5),
        compiler_params=pltpu.CompilerParams(vmem_limit_bytes=ROOM),
        name="gather_sum",
    )(own, *received)


def assemble_kernel(place_ref, keep_ref, received_ref, out_ref):
    half = keep_ref.shape[0]
    core = place_ref[1]
    out_ref[pl.ds(pl.multiple_of(core * half, half), half), :] = keep_ref[...]
    out_ref[pl.ds(pl.multiple_of((1 - core) * half, half), half), :] = received_ref[...]


def assemble(place, keep, received):
    return pl.pallas_call(
        assemble_kernel,
        out_shape=jax.ShapeDtypeStruct((2 * keep.shape[0], keep.shape[1]), keep.dtype),
        in_specs=[whole(pltpu.SMEM)] + [whole()] * 2,
        out_specs=whole(),
        cost_estimate=cost(1e5, 3e5),
        compiler_params=pltpu.CompilerParams(vmem_limit_bytes=ROOM),
        name="assemble",
    )(place, keep, received)


def fits_compact(queries, key_rows, expert_ids, w_gate):
    ctx = lax.axis_size("ctx")
    plane = math.isqrt(ctx)
    return (
        plane * plane == ctx
        and plane == 4
        and lax.axis_size("exp") == 2
        and w_gate.shape[0] == 1
        and ctx <= 2 * expert_ids.shape[1]
        and key_rows.shape == (HEAD, HEAD)
        and queries.shape[0] == HEAD
    )


def attend(queries, key_rows, value_rows, first):
    token_count = queries.shape[0]
    kv_heads = key_rows.shape[1] // 128
    q_heads = queries.shape[1] // 128
    group = q_heads // kv_heads
    grouped = queries.reshape(token_count, kv_heads, group, 128)
    query_pos = first + jnp.arange(token_count, dtype=jnp.int32)
    last_pos = first + token_count - 1
    scale = 128 ** (-0.5)
    shape_rows = (kv_heads, group, token_count)
    start_state = (
        jnp.full(shape_rows, -1e30, jnp.float32),
        jnp.zeros(shape_rows, jnp.float32),
        jnp.zeros(shape_rows + (128,), jnp.float32),
    )
    key_piece = lax.all_gather(key_rows, "ctx", axis=0, tiled=True)
    value_piece = lax.all_gather(value_rows, "ctx", axis=0, tiled=True)
    count = key_piece.shape[0]
    width = math.gcd(count, 512)

    def step(block_index, state):
        offset = block_index * width

        def compute(inner):
            running_max, running_sum, accum = inner
            key_block = lax.dynamic_slice_in_dim(key_piece, block_index * width, width, 0).reshape(
                width, kv_heads, 128
            )
            value_block = lax.dynamic_slice_in_dim(
                value_piece, block_index * width, width, 0
            ).reshape(width, kv_heads, 128)
            scores = (
                jnp.einsum("tkgd,skd->kgts", grouped, key_block, preferred_element_type=jnp.float32)
                * scale
            )
            key_pos = offset + jnp.arange(width, dtype=jnp.int32)
            allowed = key_pos[None, :] <= query_pos[:, None]
            scores = jnp.where(allowed, scores, -jnp.inf)
            new_max = jnp.maximum(running_max, jnp.max(scores, axis=-1))
            factor = jnp.exp(running_max - new_max)
            weights = jnp.exp(scores - new_max[..., None])
            new_sum = running_sum * factor + jnp.sum(weights, axis=-1)
            product = jnp.einsum(
                "kgts,skd->kgtd",
                weights.astype(jnp.bfloat16),
                value_block,
                preferred_element_type=jnp.float32,
            )
            return (new_max, new_sum, accum * factor[..., None] + product)

        return lax.cond(offset <= last_pos, compute, lambda inner: inner, state)

    _, total, accum = lax.fori_loop(0, count // width, step, start_state)
    output = accum / total[..., None]
    return (
        jnp.transpose(output, (2, 0, 1, 3)).reshape(token_count, q_heads * 128).astype(jnp.bfloat16)
    )


def place_rows(expert_ids, sent_rows, capacity, expert_count):
    top_count = expert_ids.shape[1]
    flat_ids = expert_ids.reshape(-1)
    onehot = (flat_ids[:, None] == jnp.arange(expert_count, dtype=jnp.int32)[None, :]).astype(
        jnp.int32
    )
    earlier = jnp.cumsum(onehot, axis=0) - onehot
    slot_index = jnp.sum(earlier * onehot, axis=1)
    destination = flat_ids * capacity + slot_index
    copies = jnp.repeat(sent_rows, top_count, axis=0)
    buffer = (
        jnp.zeros((expert_count * capacity, sent_rows.shape[1]), sent_rows.dtype)
        .at[destination]
        .set(copies)
    )
    return (buffer.reshape(expert_count, 2, capacity // 2, sent_rows.shape[1]), destination)


def per_device(
    queries,
    key_rows,
    value_rows,
    hidden_in,
    out_proj,
    norm_gain,
    expert_ids,
    gate_scores,
    w_gate,
    w_up,
    w_down,
):
    if fits_compact(queries, key_rows, expert_ids, w_gate):
        return compact(
            queries, key_rows, value_rows, hidden_in, out_proj, norm_gain,
            expert_ids, gate_scores, w_gate, w_up, w_down,
        )
    token_count = queries.shape[0]
    model_width = hidden_in.shape[1]
    half_width = model_width // 2
    ctx_size = lax.axis_size("ctx")
    local_experts = w_gate.shape[0]
    expert_count = local_experts * ctx_size
    top_count = expert_ids.shape[1]
    capacity = 2 * (
        min(token_count, max(2, 3 * token_count * top_count // (2 * expert_count))) // 2
    )
    half_cap = capacity // 2
    first = lax.axis_index("ctx") * token_count
    core = lax.axis_index("exp")
    side_start = core * half_width
    attended = attend(queries, key_rows, value_rows, first)
    head_part = jnp.dot(attended, out_proj, preferred_element_type=jnp.float32)
    attn_full = lax.psum(head_part.astype(jnp.bfloat16), "exp").astype(jnp.float32)
    resid = hidden_in.astype(jnp.float32) + attn_full
    inverse = lax.rsqrt(jnp.mean(resid * resid, axis=1, keepdims=True) + 1e-06)
    sent_rows = (resid * inverse * norm_gain[None, :]).astype(jnp.bfloat16)
    resid_half = lax.dynamic_slice_in_dim(resid, side_start, half_width, 1)
    buffer, destination = place_rows(expert_ids, sent_rows, capacity, expert_count)
    own_slots = lax.dynamic_slice_in_dim(buffer, core, 1, 1)
    grouped = lax.all_to_all(own_slots, "ctx", split_axis=0, concat_axis=0, tiled=True)
    gate = jnp.einsum("sxmd,xdf->sxmf", grouped, w_gate, preferred_element_type=jnp.float32)
    upper = jnp.einsum("sxmd,xdf->sxmf", grouped, w_up, preferred_element_type=jnp.float32)
    hidden = (jax.nn.silu(gate) * upper).astype(jnp.bfloat16)
    partial_value = jnp.einsum(
        "sxmf,xfd->sxmd", hidden, w_down, preferred_element_type=jnp.float32
    ).astype(jnp.bfloat16)
    returned = lax.all_to_all(partial_value, "ctx", split_axis=0, concat_axis=0, tiled=True)
    flat_back = returned.reshape(expert_count * half_cap, model_width)
    slot_of = destination % capacity
    expert_of = destination // capacity
    owned = slot_of // half_cap == core
    local_index = jnp.where(owned, expert_of * half_cap + slot_of - core * half_cap, 0)
    picked = flat_back[local_index].astype(jnp.float32)
    mixing = (gate_scores / jnp.sum(gate_scores, axis=1, keepdims=True)).reshape(-1)
    mixing = jnp.where(owned, mixing, 0.0)
    weighted = (picked * mixing[:, None]).reshape(token_count, top_count, model_width)
    mixed_part = jnp.sum(weighted, axis=1)
    moe_half = lax.psum_scatter(
        mixed_part.astype(jnp.bfloat16), "exp", scatter_dimension=1, tiled=True
    ).astype(jnp.float32)
    return (resid_half + moe_half).astype(jnp.bfloat16)


def solution(mesh):
    placed = (
        P(("groups", "ctx"), "exp"),
        P(("groups", "ctx"), "exp"),
        P(("groups", "ctx"), "exp"),
        P(("groups", "ctx"), None),
        P("exp", None),
        P(),
        P(("groups", "ctx"), None),
        P(("groups", "ctx"), None),
        P("ctx", None, None),
        P("ctx", None, None),
        P("ctx", None, None),
    )
    return jax.shard_map(
        per_device,
        mesh=mesh,
        in_specs=placed,
        out_specs=P(("groups", "ctx"), "exp"),
        check_vma=False,
    )
```

```python
import functools
import math

import jax
import jax.numpy as jnp
from jax import lax
from jax.experimental import pallas as pl
from jax.experimental.pallas import tpu as pltpu
from jax.sharding import PartitionSpec as P


HEAD = 128
LOG2E = 1.4426950408889634
HIDE = -1e30
ROOM = 20 << 20
GROUP = 512


def whole(memory_space=pltpu.VMEM):
    return pl.BlockSpec(memory_space=memory_space)


def cost(flops, size, exps=0):
    return pl.CostEstimate(flops=int(flops), bytes_accessed=int(size), transcendentals=int(exps))


def fetch_all(pairs, sems):
    copies = [
        pltpu.make_async_copy(source, target, sems.at[n])
        for n, (source, target) in enumerate(pairs)
    ]
    for copy in copies:
        copy.start()
    return copies


def held(value):
    return pltpu.with_memory_space_constraint(value, pltpu.HBM)


def pack_kernel(key_ref, value_ref, ids_ref, score_ref, rows_ref, mixed_ref, both, ids, score, sems):
    count, width = key_ref.shape
    copies = fetch_all(
        [
            (key_ref, both.at[:, :width]),
            (value_ref, both.at[:, width:]),
            (ids_ref, ids),
            (score_ref, score),
        ],
        sems,
    )
    for copy in copies:
        copy.wait()
    rows_ref[...] = both[...]
    mixed_ref[:count, :] = both[...]
    experts = mixed_ref.shape[0] - count
    mix = score[...] / jnp.sum(score[...], axis=0, keepdims=True)
    number = lax.broadcasted_iota(jnp.int32, (experts, count), 0)
    turned = jnp.zeros((experts, count), jnp.float32)
    for k in range(ids.shape[0]):
        turned = turned + jnp.where(number == ids[k : k + 1, :], mix[k : k + 1, :], 0.0)
    high = turned.astype(jnp.bfloat16)
    low = (turned - high.astype(jnp.float32)).astype(jnp.bfloat16)
    mixed_ref[count:, :] = jnp.concatenate([high, low], axis=1)


def pack(key_rows, value_rows, expert_ids, gate_scores, experts):
    count, width = key_rows.shape
    top = expert_ids.shape[1]
    return pl.pallas_call(
        pack_kernel,
        out_shape=(
            jax.ShapeDtypeStruct((count, 2 * width), jnp.bfloat16),
            jax.ShapeDtypeStruct((count + experts, 2 * width), jnp.bfloat16),
        ),
        in_specs=[whole(pltpu.HBM)] * 4,
        out_specs=(whole(), whole()),
        scratch_shapes=[
            pltpu.VMEM((count, 2 * width), jnp.bfloat16),
            pltpu.VMEM((top, count), jnp.int32),
            pltpu.VMEM((top, count), jnp.float32),
            pltpu.SemaphoreType.DMA((4,)),
        ],
        cost_estimate=cost(1e5, 3e5),
        compiler_params=pltpu.CompilerParams(vmem_limit_bytes=ROOM),
        name="pack",
    )(*[held(value) for value in (key_rows, value_rows, expert_ids.T, gate_scores.T)])


def cut_kernel(down_ref, out_ref, sem):
    half = out_ref.shape[0]
    start = pl.multiple_of(lax.axis_index("exp") * half, half)
    copy = pltpu.make_async_copy(down_ref.at[0, pl.ds(start, half)], out_ref, sem)
    copy.start()
    copy.wait()


def cut(w_down):
    _, units, model = w_down.shape
    return pl.pallas_call(
        cut_kernel,
        out_shape=jax.ShapeDtypeStruct((units // 2, model), w_down.dtype),
        in_specs=[whole(pl.ANY)],
        out_specs=whole(),
        scratch_shapes=[pltpu.SemaphoreType.DMA],
        cost_estimate=cost(1e3, 1e6),
        compiler_params=pltpu.CompilerParams(vmem_limit_bytes=ROOM),
        name="cut",
    )(held(w_down))


def merge_kernel(first_ref, second_ref, out_ref):
    out_ref[...] = first_ref[...] + second_ref[...]


def merge(first, second):
    pair = [pltpu.with_memory_space_constraint(value, pltpu.VMEM) for value in (first, second)]
    return pl.pallas_call(
        merge_kernel,
        out_shape=jax.ShapeDtypeStruct(first.shape, first.dtype),
        in_specs=[whole()] * 2,
        out_specs=whole(),
        cost_estimate=cost(1e5, 3e6),
        compiler_params=pltpu.CompilerParams(vmem_limit_bytes=ROOM),
        name="merge",
    )(*pair)


def stack_kernel(gate_ref, up_ref, mine_ref, other_ref, own_wide, swapped_wide, sems):
    units, core = gate_ref.shape[2], lax.axis_index("exp")
    mine = pl.ds(pl.multiple_of(core * units, units), units)
    other = pl.ds(pl.multiple_of((1 - core) * units, units), units)
    pairs = [
        (gate_ref.at[0], own_wide.at[:, :units]),
        (up_ref.at[0], own_wide.at[:, units:]),
        (mine_ref, swapped_wide.at[:, mine]),
        (other_ref, swapped_wide.at[:, other]),
    ]
    for copy in fetch_all(pairs, sems):
        copy.wait()


def stack(w_gate, w_up, mine, other):
    _, model, units = w_gate.shape
    return pl.pallas_call(
        stack_kernel,
        out_shape=(jax.ShapeDtypeStruct((model, 2 * units), jnp.bfloat16),) * 2,
        in_specs=[whole(pl.ANY)] * 4,
        out_specs=(whole(),) * 2,
        scratch_shapes=[pltpu.SemaphoreType.DMA((4,))],
        cost_estimate=cost(1e5, 6e6),
        compiler_params=pltpu.CompilerParams(vmem_limit_bytes=ROOM),
        name="stack",
    )(w_gate, w_up, mine, other)


def join_kernel(count, *refs):
    out_ref = refs[-1]
    tail = None
    for n, ref in enumerate(refs[:-1]):
        out_ref[n * count : (n + 1) * count, :] = ref[:count, :]
        if ref.shape[0] > count:
            tail = ref
    out_ref[(len(refs) - 1) * count :, :] = tail[count:, :]


def join(parts, count):
    total = sum(part.shape[0] for part in parts)
    return pl.pallas_call(
        functools.partial(join_kernel, count),
        out_shape=jax.ShapeDtypeStruct((total, parts[0].shape[1]), parts[0].dtype),
        in_specs=[whole()] * len(parts),
        out_specs=whole(),
        cost_estimate=cost(1e5, 4e5),
        compiler_params=pltpu.CompilerParams(vmem_limit_bytes=ROOM),
        name="join",
    )(*parts)


def soften(query, keys, values, biases, state):
    scale = HEAD ** (-0.5) * LOG2E
    scores = lax.dot_general(
        query, keys, (((1,), (1,)), ((), ())), preferred_element_type=jnp.float32
    )
    pieces = [scores[:, n * HEAD : (n + 1) * HEAD] for n in range(keys.shape[0] // HEAD)]
    if biases is not None:
        pieces = [piece + bias for piece, bias in zip(pieces, biases)]
    peak = functools.reduce(jnp.maximum, pieces)
    peak = jnp.max(peak, axis=1, keepdims=True)
    if state is not None:
        peak = jnp.maximum(peak, state[0][:, :1])
    shift = peak * scale
    weights = [jnp.exp2(piece * scale - shift) for piece in pieces]
    total = functools.reduce(jnp.add, weights)
    product = jnp.dot(
        jnp.concatenate([w.astype(jnp.bfloat16) for w in weights], axis=1),
        values,
        preferred_element_type=jnp.float32,
    )
    if state is not None:
        factor = jnp.exp2(state[0][:, :1] * scale - shift)
        total = total + state[1] * factor
        product = product + state[2] * factor
    return peak, total, product


def near_kernel(plane, heads_ref, *refs):
    sources, column_ref = refs[:plane], refs[plane]
    peak_ref, total_ref, sum_ref, keys, values = refs[plane + 1 :]
    count = HEAD
    layers = column_ref.shape[0] // count
    for n, ref in enumerate(sources):
        keys[n * count : (n + 1) * count, :] = ref[:count, :HEAD]
        values[n * count : (n + 1) * count, :] = ref[:count, HEAD:]
    keys[plane * count :, :] = column_ref[: layers * count, :HEAD]
    values[plane * count :, :] = column_ref[: layers * count, HEAD:]
    me = lax.axis_index("ctx")
    row = lax.broadcasted_iota(jnp.int32, (GROUP, count), 0) % count
    number = lax.broadcasted_iota(jnp.int32, (GROUP, count), 1)
    biases = [jnp.where(number <= row, 0.0, HIDE)]
    for step in range(1, plane):
        biases.append(jnp.where((me ^ step) < me, 0.0, HIDE))
    for step in range(1, layers + 1):
        biases.append(jnp.where(me >= step * plane, 0.0, HIDE))
    for start in range(0, heads_ref.shape[0], GROUP):
        part = slice(start, start + GROUP)
        peak, total, product = soften(heads_ref[part], keys[...], values[...], biases, None)
        peak_ref[part] = jnp.broadcast_to(peak, (GROUP, HEAD))
        total_ref[part] = total
        sum_ref[part] = product


def turn_kernel(query_ref, heads_ref, sems):
    count = query_ref.shape[0]
    pairs = []
    for head in range(query_ref.shape[1] // HEAD):
        part = slice(head * count, (head + 1) * count)
        pairs.append((query_ref.at[:, head * HEAD : (head + 1) * HEAD], heads_ref.at[part]))
    for copy in fetch_all(pairs, sems):
        copy.wait()


def turn(queries):
    count, width = queries.shape
    return pl.pallas_call(
        turn_kernel,
        out_shape=jax.ShapeDtypeStruct((count * width // HEAD, HEAD), queries.dtype),
        in_specs=[whole(pl.ANY)],
        out_specs=whole(),
        scratch_shapes=[pltpu.SemaphoreType.DMA((width // HEAD,))],
        cost_estimate=cost(1e5, 1e6),
        compiler_params=pltpu.CompilerParams(vmem_limit_bytes=ROOM),
        name="turn",
    )(held(queries))


def near(heads, sources, column, plane):
    shape = jax.ShapeDtypeStruct(heads.shape, jnp.float32)
    keys = (plane + column.shape[0] // HEAD) * HEAD
    return pl.pallas_call(
        functools.partial(near_kernel, plane),
        out_shape=(shape,) * 3,
        in_specs=[whole()] * (2 + len(sources)),
        out_specs=(whole(),) * 3,
        scratch_shapes=[pltpu.VMEM((keys, HEAD), jnp.bfloat16)] * 2,
        cost_estimate=cost(4 * heads.size * keys, 4e6, heads.shape[0] * keys),
        compiler_params=pltpu.CompilerParams(vmem_limit_bytes=ROOM),
        name="near",
    )(heads, *sources, column)


def extend(plane, query_ref, state, sources, keys, values, out):
    count = HEAD
    layers = sources[0].shape[0] // count
    height = lax.axis_index("ctx") // plane

    @pl.when(height == 0)
    def _():
        for source, target in zip(state, out):
            target[...] = source[...]

    for used in range(1, layers + 1):

        @pl.when(height == used)
        def _(used=used):
            span = used * count
            for n, ref in enumerate(sources):
                keys[n * span : (n + 1) * span, :] = ref[:span, :HEAD]
                values[n * span : (n + 1) * span, :] = ref[:span, HEAD:]
            size = len(sources) * span
            for start in range(0, query_ref.shape[0], GROUP):
                part = slice(start, start + GROUP)
                peak, total, product = soften(
                    query_ref[part],
                    keys[:size],
                    values[:size],
                    None,
                    [ref[part] for ref in state],
                )
                out[0][part] = jnp.broadcast_to(peak, (GROUP, HEAD))
                out[1][part] = total
                out[2][part] = product


def more_kernel(plane, steps, query_ref, *refs):
    state, sources, refs = refs[:3], refs[3 : 3 + steps], refs[3 + steps :]
    extend(plane, query_ref, state, sources, refs[3], refs[4], refs[:3])


def more(heads, state, sources, plane):
    shape = jax.ShapeDtypeStruct(heads.shape, jnp.float32)
    keys = len(sources) * (sources[0].shape[0] // HEAD) * HEAD
    return pl.pallas_call(
        functools.partial(more_kernel, plane, len(sources)),
        out_shape=(shape,) * 3,
        in_specs=[whole()] * (4 + len(sources)),
        out_specs=(whole(),) * 3,
        scratch_shapes=[pltpu.VMEM((keys, HEAD), jnp.bfloat16)] * 2,
        cost_estimate=cost(4 * heads.size * keys, 4e6, heads.shape[0] * keys),
        compiler_params=pltpu.CompilerParams(vmem_limit_bytes=ROOM),
        name="more",
    )(heads, *state, *sources)


def far_kernel(plane, query_ref, peak_ref, total_ref, sum_ref, source_ref, *refs):
    weight_ref, own_ref, other_ref, keys, values, peak, total, product, attended, result = refs
    state, work = (peak_ref, total_ref, sum_ref), (peak, total, product)
    extend(plane, query_ref, state, (source_ref,), keys, values, work)
    count = attended.shape[0]
    core = lax.axis_index("exp")
    for head in range(query_ref.shape[0] // count):
        part = slice(head * count, (head + 1) * count)
        denom = jnp.sum(total[part], axis=1, keepdims=True)
        attended[:, head * HEAD : (head + 1) * HEAD] = (product[part] / denom).astype(jnp.bfloat16)
    result[...] = jnp.dot(attended[...], weight_ref[...], preferred_element_type=jnp.float32)
    half = count // 2
    own_ref[...] = result[pl.ds(pl.multiple_of(core * half, half), half), :]
    other = result[pl.ds(pl.multiple_of((1 - core) * half, half), half), :]
    other_ref[...] = other.astype(jnp.bfloat16)


def far(heads, state, source, out_proj, plane):
    width, model = out_proj.shape
    count = heads.size // width
    keys = source.shape[0] // HEAD * HEAD
    return pl.pallas_call(
        functools.partial(far_kernel, plane),
        out_shape=(
            jax.ShapeDtypeStruct((count // 2, model), jnp.float32),
            jax.ShapeDtypeStruct((count // 2, model), jnp.bfloat16),
        ),
        in_specs=[whole()] * 6,
        out_specs=(whole(),) * 2,
        scratch_shapes=[pltpu.VMEM((keys, HEAD), jnp.bfloat16)] * 2
        + [pltpu.VMEM(heads.shape, jnp.float32)] * 3
        + [
            pltpu.VMEM((count, width), jnp.bfloat16),
            pltpu.VMEM((count, model), jnp.float32),
        ],
        cost_estimate=cost(
            4 * heads.size * keys + 2 * count * width * model, 6e6, heads.shape[0] * keys
        ),
        compiler_params=pltpu.CompilerParams(vmem_limit_bytes=ROOM),
        name="far",
    )(heads, *state, source, out_proj)


def norm_kernel(hidden_ref, own_ref, other_ref, gain_ref, resid_ref, normed_ref):
    half = own_ref.shape[0]
    start = pl.multiple_of(lax.axis_index("exp") * half, half)
    hidden = hidden_ref[pl.ds(start, half), :].astype(jnp.float32)
    resid = hidden + own_ref[...] + other_ref[...].astype(jnp.float32)
    inverse = lax.rsqrt(jnp.mean(resid * resid, axis=1, keepdims=True) + 1e-06)
    resid_ref[...] = resid
    normed_ref[...] = (resid * inverse * gain_ref[...]).astype(jnp.bfloat16)


def norm(hidden_in, own, other, norm_gain):
    return pl.pallas_call(
        norm_kernel,
        out_shape=(
            jax.ShapeDtypeStruct(own.shape, jnp.float32),
            jax.ShapeDtypeStruct(own.shape, jnp.bfloat16),
        ),
        in_specs=[whole()] * 4,
        out_specs=(whole(),) * 2,
        cost_estimate=cost(1e6, 1e6),
        compiler_params=pltpu.CompilerParams(vmem_limit_bytes=ROOM),
        name="norm",
    )(hidden_in, own, other, norm_gain)


def share_kernel(plane, *refs):
    pieces, out_ref, turned = refs[:-2], refs[-2], refs[-1]
    me = lax.axis_index("ctx")
    experts, count = pieces[0].shape[0], pieces[0].shape[1] // 2
    half = count // 2
    start = pl.multiple_of(lax.axis_index("exp") * half, half)
    number = lax.broadcasted_iota(jnp.int32, (experts, count), 0)
    lane = lax.broadcasted_iota(jnp.int32, (count, count), 1)
    diagonal = lax.broadcasted_iota(jnp.int32, (count, count), 0) == lane
    for n, piece in enumerate(pieces):
        mix = piece[:, :count].astype(jnp.float32) + piece[:, count:].astype(jnp.float32)
        columns = jnp.zeros((count, count), jnp.float32)
        for side in range(2):
            line = jnp.sum(
                jnp.where(number == (me if side == 0 else me ^ plane), mix, 0.0), axis=0, keepdims=True
            )
            column = jnp.sum(jnp.where(diagonal, line, 0.0), axis=1, keepdims=True)
            columns = jnp.where(lane == side, column, columns)
        turned[...] = columns
        out_ref[n * half : (n + 1) * half, :] = turned[pl.ds(start, half), :]


def share(pieces, experts, plane):
    width = pieces[0].shape[1]
    count = width // 2
    specs = []
    for piece in pieces:
        block = piece.shape[0] // experts - 1
        specs.append(pl.BlockSpec((experts, width), lambda i, block=block: (block, 0)))
    rows = len(pieces) * count // 2
    return pl.pallas_call(
        functools.partial(share_kernel, plane),
        grid=(1,),
        out_shape=jax.ShapeDtypeStruct((rows, count), jnp.float32),
        in_specs=specs,
        out_specs=pl.BlockSpec((rows, count), lambda i: (0, 0)),
        scratch_shapes=[pltpu.VMEM((count, count), jnp.float32)],
        cost_estimate=cost(1e6, 4e5),
        compiler_params=pltpu.CompilerParams(vmem_limit_bytes=ROOM),
        name="columns",
    )(*pieces)


def expert_rows(share_ref, first, inputs, wide_refs, rows, hidden):
    size = inputs[0].shape[0]
    units = wide_refs[0].shape[1] // 2
    for n, ref in enumerate(inputs):
        rows[n * size : (n + 1) * size, :] = ref[...]
    for side, wide_ref in enumerate(wide_refs):
        both = jnp.dot(rows[...], wide_ref[...], preferred_element_type=jnp.float32)
        gate, upper = both[:, :units], both[:, units:]
        factor = share_ref[first * size : (first + len(inputs)) * size, side : side + 1]
        value = gate / (1.0 + jnp.exp(-gate)) * upper * factor
        hidden[:, side * units : (side + 1) * units] = value.astype(jnp.bfloat16)


def expert_sums(hidden, tall_ref, outputs):
    size = outputs[0].shape[0]
    total = jnp.dot(hidden[...], tall_ref[...], preferred_element_type=jnp.float32)
    for n, ref in enumerate(outputs):
        ref[...] = total[n * size : (n + 1) * size, :].astype(ref.dtype)


def expand_kernel(share_ref, *refs):
    inputs, wide_refs, hidden, rows = refs[:-4], refs[-4:-2], refs[-2], refs[-1]
    expert_rows(share_ref, 0, inputs, wide_refs, rows, hidden)


def expand(shares, inputs, wide):
    blocks = len(inputs)
    size, model = inputs[0].shape
    both = wide[0].shape[1]
    return pl.pallas_call(
        expand_kernel,
        out_shape=jax.ShapeDtypeStruct((blocks * size, both), jnp.bfloat16),
        in_specs=[whole()] * (3 + blocks),
        out_specs=whole(),
        scratch_shapes=[pltpu.VMEM((blocks * size, model), jnp.bfloat16)],
        cost_estimate=cost(4 * blocks * size * model * both, 4 * model * both),
        compiler_params=pltpu.CompilerParams(vmem_limit_bytes=ROOM),
        name="expand",
    )(shares, *inputs, *wide)


def contract_kernel(hidden_ref, down_ref, mine_ref, other_ref, *refs):
    outputs, tall_ref, sems = refs[:-2], refs[-2], refs[-1]
    units, core = down_ref.shape[1], lax.axis_index("exp")
    half = units // 2
    mine = pl.ds(pl.multiple_of(units + core * half, half), half)
    other = pl.ds(pl.multiple_of(units + (1 - core) * half, half), half)
    pairs = [
        (down_ref.at[0], tall_ref.at[:units]),
        (mine_ref, tall_ref.at[mine]),
        (other_ref, tall_ref.at[other]),
    ]
    for copy in fetch_all(pairs, sems):
        copy.wait()
    expert_sums(hidden_ref, tall_ref, outputs)


def contract(hidden, w_down, mine, other, dtypes):
    blocks = len(dtypes)
    size, model = hidden.shape[0] // blocks, w_down.shape[2]
    both = hidden.shape[1]
    return pl.pallas_call(
        contract_kernel,
        out_shape=tuple(jax.ShapeDtypeStruct((size, model), dtype) for dtype in dtypes)
        + (jax.ShapeDtypeStruct((both, model), jnp.bfloat16),),
        in_specs=[whole()] + [whole(pl.ANY)] * 3,
        out_specs=(whole(),) * (blocks + 1),
        scratch_shapes=[pltpu.SemaphoreType.DMA((3,))],
        cost_estimate=cost(2 * blocks * size * model * both, 2 * model * both),
        compiler_params=pltpu.CompilerParams(vmem_limit_bytes=ROOM),
        name="contract",
    )(hidden, w_down, mine, other)


def expert_far_kernel(first, blocks, share_ref, *refs):
    inputs, wide_refs, tall_ref = refs[:blocks], refs[blocks : blocks + 2], refs[blocks + 2]
    outputs, rows, hidden = refs[blocks + 3 : -2], refs[-2], refs[-1]
    expert_rows(share_ref, first, inputs, wide_refs, rows, hidden)
    expert_sums(hidden, tall_ref, outputs)


def experts_far(shares, inputs, wide, tall, first):
    blocks = len(inputs)
    size, model = inputs[0].shape
    both = tall.shape[0]
    return pl.pallas_call(
        functools.partial(expert_far_kernel, first, blocks),
        out_shape=(jax.ShapeDtypeStruct((size, model), jnp.bfloat16),) * blocks,
        in_specs=[whole()] * (4 + blocks),
        out_specs=(whole(),) * blocks,
        scratch_shapes=[
            pltpu.VMEM((blocks * size, model), jnp.bfloat16),
            pltpu.VMEM((blocks * size, both), jnp.bfloat16),
        ],
        cost_estimate=cost(6 * blocks * size * model * both, 6 * model * both),
        compiler_params=pltpu.CompilerParams(vmem_limit_bytes=ROOM),
        name="experts_far",
    )(shares, *inputs, *wide, tall)


def final_kernel(resid_ref, own_ref, *refs):
    keep_ref, send_ref, work = refs[-3:]
    total = own_ref[...]
    for ref in refs[:-3]:
        total = total + ref[...].astype(jnp.float32)
    work[...] = (resid_ref[...] + total).astype(jnp.bfloat16)
    half = keep_ref.shape[1]
    core = lax.axis_index("exp")
    keep_ref[...] = work[:, pl.ds(pl.multiple_of(core * half, half), half)]
    send_ref[...] = work[:, pl.ds(pl.multiple_of((1 - core) * half, half), half)]


def final(resid, own, received):
    rows, model = resid.shape
    shape = jax.ShapeDtypeStruct((rows, model // 2), jnp.bfloat16)
    return pl.pallas_call(
        final_kernel,
        out_shape=(shape, shape),
        in_specs=[whole()] * (2 + len(received)),
        out_specs=(whole(),) * 2,
        scratch_shapes=[pltpu.VMEM((rows, model), jnp.bfloat16)],
        cost_estimate=cost(1e6, 1e6),
        compiler_params=pltpu.CompilerParams(vmem_limit_bytes=ROOM),
        name="final",
    )(resid, own, *received)


def compact(
    queries,
    key_rows,
    value_rows,
    hidden_in,
    out_proj,
    norm_gain,
    expert_ids,
    gate_scores,
    w_gate,
    w_up,
    w_down,
):
    count = queries.shape[0]
    model = hidden_in.shape[1]
    ctx = lax.axis_size("ctx")
    plane = math.isqrt(ctx)
    planes = ctx // plane
    away = 2 * plane


    def flip(value, mask):
        return lax.ppermute(value, "ctx", [(i, i ^ mask) for i in range(ctx)])

    def upward(value, step):
        return lax.ppermute(value, "ctx", [(i, i + step) for i in range(ctx - step)])

    def across(value):
        return lax.ppermute(value, "exp", [(0, 1), (1, 0)])

    mates = range(1, plane)
    rows, mixed = pack(key_rows, value_rows, expert_ids, gate_scores, w_gate.shape[0] * ctx)
    column = [
        flip(mixed, away)
        if step == 2
        else upward(rows, step * plane)
        for step in range(1, planes)
    ]
    level = [flip(mixed, mate) for mate in mates]
    joined = join(column, count)
    corner = [flip(joined, mate) for mate in mates]

    def half_flip(value, side):
        pairs = [(2 * i + side, 2 * (i ^ plane) + side) for i in range(ctx)]
        return lax.ppermute(value, ("ctx", "exp"), pairs)

    gate_swap = half_flip(w_gate[0], 0)
    up_swap = half_flip(w_up[0], 1)
    tall = cut(w_down)
    tall_swap = flip(tall, plane)

    heads = turn(queries)
    state = near(heads, [mixed] + level, joined, plane)
    state = more(heads, state, corner[:-1], plane)
    own, other = far(heads, state, corner[-1], out_proj, plane)
    resid, normed = norm(hidden_in, own, across(other), norm_gain.reshape(1, model))
    wide_swap = merge(gate_swap, up_swap)
    wide = stack(w_gate, w_up, wide_swap, across(wide_swap))
    shares = share([mixed] + level + [joined] + corner, w_gate.shape[0] * ctx, plane)
    opposite = flip(normed, away)
    level_rows = [flip(normed, mate) for mate in mates]
    corner_rows = [flip(opposite, mate) for mate in mates]
    f32, bf16 = jnp.float32, jnp.bfloat16
    hidden = expand(shares, [normed] + level_rows + [opposite], wide)
    *near_out, tall = contract(
        hidden, w_down, tall_swap, across(tall_swap),
        [f32] + [bf16] * len(mates) + [f32],
    )
    far_out = experts_far(shares, corner_rows, wide, tall, plane + 1)
    passed = [flip(value, mate) for value, mate in zip(far_out, mates)]
    direct = [flip(value, mate) for value, mate in zip(near_out[1:plane], mates)]
    last = flip(gather_sum(near_out[plane], passed), away)
    keep, send = final(resid, near_out[0], direct + [last])
    return assemble(keep, across(send))


def gather_sum_kernel(own_ref, *refs):
    total = own_ref[...]
    for ref in refs[:-1]:
        total = total + ref[...].astype(jnp.float32)
    refs[-1][...] = total.astype(jnp.bfloat16)


def gather_sum(own, received):
    return pl.pallas_call(
        gather_sum_kernel,
        out_shape=jax.ShapeDtypeStruct(own.shape, jnp.bfloat16),
        in_specs=[whole()] * (1 + len(received)),
        out_specs=whole(),
        cost_estimate=cost(1e5, 8e5),
        compiler_params=pltpu.CompilerParams(vmem_limit_bytes=ROOM),
        name="gather_sum",
    )(own, *received)


def assemble_kernel(keep_ref, received_ref, out_ref):
    half = keep_ref.shape[0]
    core = lax.axis_index("exp")
    out_ref[pl.ds(pl.multiple_of(core * half, half), half), :] = keep_ref[...]
    out_ref[pl.ds(pl.multiple_of((1 - core) * half, half), half), :] = received_ref[...]


def assemble(keep, received):
    return pl.pallas_call(
        assemble_kernel,
        out_shape=jax.ShapeDtypeStruct((2 * keep.shape[0], keep.shape[1]), keep.dtype),
        in_specs=[whole()] * 2,
        out_specs=whole(),
        cost_estimate=cost(1e5, 3e5),
        compiler_params=pltpu.CompilerParams(vmem_limit_bytes=ROOM),
        name="assemble",
    )(keep, received)


def fits_compact(queries, key_rows, expert_ids, w_gate):
    ctx = lax.axis_size("ctx")
    plane = math.isqrt(ctx)
    return (
        plane * plane == ctx
        and plane == 4
        and lax.axis_size("exp") == 2
        and w_gate.shape[0] == 1
        and ctx <= 2 * expert_ids.shape[1]
        and key_rows.shape == (HEAD, HEAD)
        and queries.shape[0] == HEAD
    )


def attend(queries, key_rows, value_rows, first):
    token_count = queries.shape[0]
    kv_heads = key_rows.shape[1] // 128
    q_heads = queries.shape[1] // 128
    group = q_heads // kv_heads
    grouped = queries.reshape(token_count, kv_heads, group, 128)
    query_pos = first + jnp.arange(token_count, dtype=jnp.int32)
    last_pos = first + token_count - 1
    scale = 128 ** (-0.5)
    shape_rows = (kv_heads, group, token_count)
    start_state = (
        jnp.full(shape_rows, -1e30, jnp.float32),
        jnp.zeros(shape_rows, jnp.float32),
        jnp.zeros(shape_rows + (128,), jnp.float32),
    )
    key_piece = lax.all_gather(key_rows, "ctx", axis=0, tiled=True)
    value_piece = lax.all_gather(value_rows, "ctx", axis=0, tiled=True)
    count = key_piece.shape[0]
    width = math.gcd(count, 512)

    def step(block_index, state):
        offset = block_index * width

        def compute(inner):
            running_max, running_sum, accum = inner
            key_block = lax.dynamic_slice_in_dim(key_piece, block_index * width, width, 0).reshape(
                width, kv_heads, 128
            )
            value_block = lax.dynamic_slice_in_dim(
                value_piece, block_index * width, width, 0
            ).reshape(width, kv_heads, 128)
            scores = (
                jnp.einsum("tkgd,skd->kgts", grouped, key_block, preferred_element_type=jnp.float32)
                * scale
            )
            key_pos = offset + jnp.arange(width, dtype=jnp.int32)
            allowed = key_pos[None, :] <= query_pos[:, None]
            scores = jnp.where(allowed, scores, -jnp.inf)
            new_max = jnp.maximum(running_max, jnp.max(scores, axis=-1))
            factor = jnp.exp(running_max - new_max)
            weights = jnp.exp(scores - new_max[..., None])
            new_sum = running_sum * factor + jnp.sum(weights, axis=-1)
            product = jnp.einsum(
                "kgts,skd->kgtd",
                weights.astype(jnp.bfloat16),
                value_block,
                preferred_element_type=jnp.float32,
            )
            return (new_max, new_sum, accum * factor[..., None] + product)

        return lax.cond(offset <= last_pos, compute, lambda inner: inner, state)

    _, total, accum = lax.fori_loop(0, count // width, step, start_state)
    output = accum / total[..., None]
    return (
        jnp.transpose(output, (2, 0, 1, 3)).reshape(token_count, q_heads * 128).astype(jnp.bfloat16)
    )


def place_rows(expert_ids, sent_rows, capacity, expert_count):
    top_count = expert_ids.shape[1]
    flat_ids = expert_ids.reshape(-1)
    onehot = (flat_ids[:, None] == jnp.arange(expert_count, dtype=jnp.int32)[None, :]).astype(
        jnp.int32
    )
    earlier = jnp.cumsum(onehot, axis=0) - onehot
    slot_index = jnp.sum(earlier * onehot, axis=1)
    destination = flat_ids * capacity + slot_index
    copies = jnp.repeat(sent_rows, top_count, axis=0)
    buffer = (
        jnp.zeros((expert_count * capacity, sent_rows.shape[1]), sent_rows.dtype)
        .at[destination]
        .set(copies)
    )
    return (buffer.reshape(expert_count, 2, capacity // 2, sent_rows.shape[1]), destination)


def per_device(
    queries,
    key_rows,
    value_rows,
    hidden_in,
    out_proj,
    norm_gain,
    expert_ids,
    gate_scores,
    w_gate,
    w_up,
    w_down,
):
    if fits_compact(queries, key_rows, expert_ids, w_gate):
        return compact(
            queries, key_rows, value_rows, hidden_in, out_proj, norm_gain,
            expert_ids, gate_scores, w_gate, w_up, w_down,
        )
    token_count = queries.shape[0]
    model_width = hidden_in.shape[1]
    half_width = model_width // 2
    ctx_size = lax.axis_size("ctx")
    local_experts = w_gate.shape[0]
    expert_count = local_experts * ctx_size
    top_count = expert_ids.shape[1]
    capacity = 2 * (
        min(token_count, max(2, 3 * token_count * top_count // (2 * expert_count))) // 2
    )
    half_cap = capacity // 2
    first = lax.axis_index("ctx") * token_count
    core = lax.axis_index("exp")
    side_start = core * half_width
    attended = attend(queries, key_rows, value_rows, first)
    head_part = jnp.dot(attended, out_proj, preferred_element_type=jnp.float32)
    attn_full = lax.psum(head_part.astype(jnp.bfloat16), "exp").astype(jnp.float32)
    resid = hidden_in.astype(jnp.float32) + attn_full
    inverse = lax.rsqrt(jnp.mean(resid * resid, axis=1, keepdims=True) + 1e-06)
    sent_rows = (resid * inverse * norm_gain[None, :]).astype(jnp.bfloat16)
    resid_half = lax.dynamic_slice_in_dim(resid, side_start, half_width, 1)
    buffer, destination = place_rows(expert_ids, sent_rows, capacity, expert_count)
    own_slots = lax.dynamic_slice_in_dim(buffer, core, 1, 1)
    grouped = lax.all_to_all(own_slots, "ctx", split_axis=0, concat_axis=0, tiled=True)
    gate = jnp.einsum("sxmd,xdf->sxmf", grouped, w_gate, preferred_element_type=jnp.float32)
    upper = jnp.einsum("sxmd,xdf->sxmf", grouped, w_up, preferred_element_type=jnp.float32)
    hidden = (jax.nn.silu(gate) * upper).astype(jnp.bfloat16)
    partial_value = jnp.einsum(
        "sxmf,xfd->sxmd", hidden, w_down, preferred_element_type=jnp.float32
    ).astype(jnp.bfloat16)
    returned = lax.all_to_all(partial_value, "ctx", split_axis=0, concat_axis=0, tiled=True)
    flat_back = returned.reshape(expert_count * half_cap, model_width)
    slot_of = destination % capacity
    expert_of = destination // capacity
    owned = slot_of // half_cap == core
    local_index = jnp.where(owned, expert_of * half_cap + slot_of - core * half_cap, 0)
    picked = flat_back[local_index].astype(jnp.float32)
    mixing = (gate_scores / jnp.sum(gate_scores, axis=1, keepdims=True)).reshape(-1)
    mixing = jnp.where(owned, mixing, 0.0)
    weighted = (picked * mixing[:, None]).reshape(token_count, top_count, model_width)
    mixed_part = jnp.sum(weighted, axis=1)
    moe_half = lax.psum_scatter(
        mixed_part.astype(jnp.bfloat16), "exp", scatter_dimension=1, tiled=True
    ).astype(jnp.float32)
    return (resid_half + moe_half).astype(jnp.bfloat16)


def solution(mesh):
    placed = (
        P(("groups", "ctx"), "exp"),
        P(("groups", "ctx"), "exp"),
        P(("groups", "ctx"), "exp"),
        P(("groups", "ctx"), None),
        P("exp", None),
        P(),
        P(("groups", "ctx"), None),
        P(("groups", "ctx"), None),
        P("ctx", None, None),
        P("ctx", None, None),
        P("ctx", None, None),
    )
    return jax.shard_map(
        per_device,
        mesh=mesh,
        in_specs=placed,
        out_specs=P(("groups", "ctx"), "exp"),
        check_vma=False,
    )
```

```python
import functools
import math

import jax
import jax.numpy as jnp
from jax import lax
from jax.experimental import pallas as pl
from jax.experimental.pallas import tpu as pltpu
from jax.sharding import PartitionSpec as P


HEAD = 128
LOG2E = 1.4426950408889634
HIDE = -1e30
ROOM = 20 << 20
GROUP = 512


def whole(memory_space=pltpu.VMEM):
    return pl.BlockSpec(memory_space=memory_space)


def cost(flops, size, exps=0):
    return pl.CostEstimate(flops=int(flops), bytes_accessed=int(size), transcendentals=int(exps))


def fetch_all(pairs, sems):
    copies = [
        pltpu.make_async_copy(source, target, sems.at[n])
        for n, (source, target) in enumerate(pairs)
    ]
    for copy in copies:
        copy.start()
    return copies


def held(value):
    return pltpu.with_memory_space_constraint(value, pltpu.HBM)


def pack_kernel(key_ref, value_ref, ids_ref, score_ref, rows_ref, mixed_ref, both, ids, score, sems):
    count, width = key_ref.shape
    copies = fetch_all(
        [
            (key_ref, both.at[:, :width]),
            (value_ref, both.at[:, width:]),
            (ids_ref, ids),
            (score_ref, score),
        ],
        sems,
    )
    for copy in copies:
        copy.wait()
    rows_ref[...] = both[...]
    mixed_ref[:count, :] = both[...]
    experts = mixed_ref.shape[0] - count
    mix = score[...] / jnp.sum(score[...], axis=0, keepdims=True)
    number = lax.broadcasted_iota(jnp.int32, (experts, count), 0)
    turned = jnp.zeros((experts, count), jnp.float32)
    for k in range(ids.shape[0]):
        turned = turned + jnp.where(number == ids[k : k + 1, :], mix[k : k + 1, :], 0.0)
    high = turned.astype(jnp.bfloat16)
    low = (turned - high.astype(jnp.float32)).astype(jnp.bfloat16)
    mixed_ref[count:, :] = jnp.concatenate([high, low], axis=1)


def pack(key_rows, value_rows, expert_ids, gate_scores, experts):
    count, width = key_rows.shape
    top = expert_ids.shape[1]
    return pl.pallas_call(
        pack_kernel,
        out_shape=(
            jax.ShapeDtypeStruct((count, 2 * width), jnp.bfloat16),
            jax.ShapeDtypeStruct((count + experts, 2 * width), jnp.bfloat16),
        ),
        in_specs=[whole(pltpu.HBM)] * 4,
        out_specs=(whole(), whole()),
        scratch_shapes=[
            pltpu.VMEM((count, 2 * width), jnp.bfloat16),
            pltpu.VMEM((top, count), jnp.int32),
            pltpu.VMEM((top, count), jnp.float32),
            pltpu.SemaphoreType.DMA((4,)),
        ],
        cost_estimate=cost(1e5, 3e5),
        compiler_params=pltpu.CompilerParams(vmem_limit_bytes=ROOM),
        name="pack",
    )(*[held(value) for value in (key_rows, value_rows, expert_ids.T, gate_scores.T)])


def cut_kernel(down_ref, first_ref, second_ref, sems):
    size = first_ref.shape[0]
    half = size + second_ref.shape[0]
    start = lax.axis_index("exp") * half
    first = pl.ds(pl.multiple_of(start, size), size)
    second = pl.ds(pl.multiple_of(start + size, size), half - size)
    pairs = [(down_ref.at[0, first], first_ref), (down_ref.at[0, second], second_ref)]
    for copy in fetch_all(pairs, sems):
        copy.wait()


def cut(w_down):
    _, units, model = w_down.shape
    size = units // 6
    return pl.pallas_call(
        cut_kernel,
        out_shape=(
            jax.ShapeDtypeStruct((size, model), w_down.dtype),
            jax.ShapeDtypeStruct((2 * size, model), w_down.dtype),
        ),
        in_specs=[whole(pl.ANY)],
        out_specs=(whole(),) * 2,
        scratch_shapes=[pltpu.SemaphoreType.DMA((2,))],
        cost_estimate=cost(1e3, 1e6),
        compiler_params=pltpu.CompilerParams(vmem_limit_bytes=ROOM),
        name="cut",
    )(held(w_down))


def merge_kernel(first_ref, second_ref, out_ref):
    out_ref[...] = first_ref[...] + second_ref[...]


def merge(first, second):
    pair = [pltpu.with_memory_space_constraint(value, pltpu.VMEM) for value in (first, second)]
    return pl.pallas_call(
        merge_kernel,
        out_shape=jax.ShapeDtypeStruct(first.shape, first.dtype),
        in_specs=[whole()] * 2,
        out_specs=whole(),
        cost_estimate=cost(1e5, 3e6),
        compiler_params=pltpu.CompilerParams(vmem_limit_bytes=ROOM),
        name="merge",
    )(*pair)


def stack_kernel(gate_ref, up_ref, mine_ref, other_ref, own_wide, swapped_wide, sems):
    units, core = gate_ref.shape[2], lax.axis_index("exp")
    mine = pl.ds(pl.multiple_of(core * units, units), units)
    other = pl.ds(pl.multiple_of((1 - core) * units, units), units)
    pairs = [
        (gate_ref.at[0], own_wide.at[:, :units]),
        (up_ref.at[0], own_wide.at[:, units:]),
        (mine_ref, swapped_wide.at[:, mine]),
        (other_ref, swapped_wide.at[:, other]),
    ]
    for copy in fetch_all(pairs, sems):
        copy.wait()


def stack(w_gate, w_up, mine, other):
    _, model, units = w_gate.shape
    return pl.pallas_call(
        stack_kernel,
        out_shape=(jax.ShapeDtypeStruct((model, 2 * units), jnp.bfloat16),) * 2,
        in_specs=[whole(pl.ANY)] * 4,
        out_specs=(whole(),) * 2,
        scratch_shapes=[pltpu.SemaphoreType.DMA((4,))],
        cost_estimate=cost(1e5, 6e6),
        compiler_params=pltpu.CompilerParams(vmem_limit_bytes=ROOM),
        name="stack",
    )(w_gate, w_up, mine, other)


def join_kernel(count, *refs):
    out_ref = refs[-1]
    tail = None
    for n, ref in enumerate(refs[:-1]):
        out_ref[n * count : (n + 1) * count, :] = ref[:count, :]
        if ref.shape[0] > count:
            tail = ref
    out_ref[(len(refs) - 1) * count :, :] = tail[count:, :]


def join(parts, count):
    total = sum(part.shape[0] for part in parts)
    return pl.pallas_call(
        functools.partial(join_kernel, count),
        out_shape=jax.ShapeDtypeStruct((total, parts[0].shape[1]), parts[0].dtype),
        in_specs=[whole()] * len(parts),
        out_specs=whole(),
        cost_estimate=cost(1e5, 4e5),
        compiler_params=pltpu.CompilerParams(vmem_limit_bytes=ROOM),
        name="join",
    )(*parts)


def soften(query, keys, values, biases, state):
    scale = HEAD ** (-0.5) * LOG2E
    scores = lax.dot_general(
        query, keys, (((1,), (1,)), ((), ())), preferred_element_type=jnp.float32
    )
    pieces = [scores[:, n * HEAD : (n + 1) * HEAD] for n in range(keys.shape[0] // HEAD)]
    if biases is not None:
        pieces = [piece + bias for piece, bias in zip(pieces, biases)]
    peak = functools.reduce(jnp.maximum, pieces)
    peak = jnp.max(peak, axis=1, keepdims=True)
    if state is not None:
        peak = jnp.maximum(peak, state[0][:, :1])
    shift = peak * scale
    weights = [jnp.exp2(piece * scale - shift) for piece in pieces]
    total = functools.reduce(jnp.add, weights)
    product = jnp.dot(
        jnp.concatenate([w.astype(jnp.bfloat16) for w in weights], axis=1),
        values,
        preferred_element_type=jnp.float32,
    )
    if state is not None:
        factor = jnp.exp2(state[0][:, :1] * scale - shift)
        total = total + state[1] * factor
        product = product + state[2] * factor
    return peak, total, product


def near_kernel(plane, heads_ref, *refs):
    sources, column_ref = refs[:plane], refs[plane]
    peak_ref, total_ref, sum_ref, keys, values = refs[plane + 1 :]
    count = HEAD
    layers = column_ref.shape[0] // count
    for n, ref in enumerate(sources):
        keys[n * count : (n + 1) * count, :] = ref[:count, :HEAD]
        values[n * count : (n + 1) * count, :] = ref[:count, HEAD:]
    keys[plane * count :, :] = column_ref[: layers * count, :HEAD]
    values[plane * count :, :] = column_ref[: layers * count, HEAD:]
    me = lax.axis_index("ctx")
    row = lax.broadcasted_iota(jnp.int32, (GROUP, count), 0) % count
    number = lax.broadcasted_iota(jnp.int32, (GROUP, count), 1)
    biases = [jnp.where(number <= row, 0.0, HIDE)]
    for step in range(1, plane):
        biases.append(jnp.where((me ^ step) < me, 0.0, HIDE))
    for step in range(1, layers + 1):
        biases.append(jnp.where(me >= step * plane, 0.0, HIDE))
    for start in range(0, heads_ref.shape[0], GROUP):
        part = slice(start, start + GROUP)
        peak, total, product = soften(heads_ref[part], keys[...], values[...], biases, None)
        peak_ref[part] = jnp.broadcast_to(peak, (GROUP, HEAD))
        total_ref[part] = total
        sum_ref[part] = product


def turn_kernel(query_ref, heads_ref, sems):
    count = query_ref.shape[0]
    pairs = []
    for head in range(query_ref.shape[1] // HEAD):
        part = slice(head * count, (head + 1) * count)
        pairs.append((query_ref.at[:, head * HEAD : (head + 1) * HEAD], heads_ref.at[part]))
    for copy in fetch_all(pairs, sems):
        copy.wait()


def turn(queries):
    count, width = queries.shape
    return pl.pallas_call(
        turn_kernel,
        out_shape=jax.ShapeDtypeStruct((count * width // HEAD, HEAD), queries.dtype),
        in_specs=[whole(pl.ANY)],
        out_specs=whole(),
        scratch_shapes=[pltpu.SemaphoreType.DMA((width // HEAD,))],
        cost_estimate=cost(1e5, 1e6),
        compiler_params=pltpu.CompilerParams(vmem_limit_bytes=ROOM),
        name="turn",
    )(held(queries))


def near(heads, sources, column, plane):
    shape = jax.ShapeDtypeStruct(heads.shape, jnp.float32)
    keys = (plane + column.shape[0] // HEAD) * HEAD
    return pl.pallas_call(
        functools.partial(near_kernel, plane),
        out_shape=(shape,) * 3,
        in_specs=[whole()] * (2 + len(sources)),
        out_specs=(whole(),) * 3,
        scratch_shapes=[pltpu.VMEM((keys, HEAD), jnp.bfloat16)] * 2,
        cost_estimate=cost(4 * heads.size * keys, 4e6, heads.shape[0] * keys),
        compiler_params=pltpu.CompilerParams(vmem_limit_bytes=ROOM),
        name="near",
    )(heads, *sources, column)


def extend(plane, query_ref, state, sources, keys, values, out):
    count = HEAD
    layers = sources[0].shape[0] // count
    height = lax.axis_index("ctx") // plane

    @pl.when(height == 0)
    def _():
        for source, target in zip(state, out):
            target[...] = source[...]

    for used in range(1, layers + 1):

        @pl.when(height == used)
        def _(used=used):
            span = used * count
            for n, ref in enumerate(sources):
                keys[n * span : (n + 1) * span, :] = ref[:span, :HEAD]
                values[n * span : (n + 1) * span, :] = ref[:span, HEAD:]
            size = len(sources) * span
            for start in range(0, query_ref.shape[0], GROUP):
                part = slice(start, start + GROUP)
                peak, total, product = soften(
                    query_ref[part],
                    keys[:size],
                    values[:size],
                    None,
                    [ref[part] for ref in state],
                )
                out[0][part] = jnp.broadcast_to(peak, (GROUP, HEAD))
                out[1][part] = total
                out[2][part] = product


def more_kernel(plane, steps, query_ref, *refs):
    state, sources, refs = refs[:3], refs[3 : 3 + steps], refs[3 + steps :]
    extend(plane, query_ref, state, sources, refs[3], refs[4], refs[:3])


def more(heads, state, sources, plane):
    shape = jax.ShapeDtypeStruct(heads.shape, jnp.float32)
    keys = len(sources) * (sources[0].shape[0] // HEAD) * HEAD
    return pl.pallas_call(
        functools.partial(more_kernel, plane, len(sources)),
        out_shape=(shape,) * 3,
        in_specs=[whole()] * (4 + len(sources)),
        out_specs=(whole(),) * 3,
        scratch_shapes=[pltpu.VMEM((keys, HEAD), jnp.bfloat16)] * 2,
        cost_estimate=cost(4 * heads.size * keys, 4e6, heads.shape[0] * keys),
        compiler_params=pltpu.CompilerParams(vmem_limit_bytes=ROOM),
        name="more",
    )(heads, *state, *sources)


def far_kernel(plane, query_ref, peak_ref, total_ref, sum_ref, source_ref, *refs):
    weight_ref, own_ref, other_ref, keys, values, peak, total, product, attended, result = refs
    state, work = (peak_ref, total_ref, sum_ref), (peak, total, product)
    extend(plane, query_ref, state, (source_ref,), keys, values, work)
    count = attended.shape[0]
    core = lax.axis_index("exp")
    for head in range(query_ref.shape[0] // count):
        part = slice(head * count, (head + 1) * count)
        denom = jnp.sum(total[part], axis=1, keepdims=True)
        attended[:, head * HEAD : (head + 1) * HEAD] = (product[part] / denom).astype(jnp.bfloat16)
    result[...] = jnp.dot(attended[...], weight_ref[...], preferred_element_type=jnp.float32)
    half = count // 2
    own_ref[...] = result[pl.ds(pl.multiple_of(core * half, half), half), :]
    other = result[pl.ds(pl.multiple_of((1 - core) * half, half), half), :]
    other_ref[...] = other.astype(jnp.bfloat16)


def far(heads, state, source, out_proj, plane):
    width, model = out_proj.shape
    count = heads.size // width
    keys = source.shape[0] // HEAD * HEAD
    return pl.pallas_call(
        functools.partial(far_kernel, plane),
        out_shape=(
            jax.ShapeDtypeStruct((count // 2, model), jnp.float32),
            jax.ShapeDtypeStruct((count // 2, model), jnp.bfloat16),
        ),
        in_specs=[whole()] * 6,
        out_specs=(whole(),) * 2,
        scratch_shapes=[pltpu.VMEM((keys, HEAD), jnp.bfloat16)] * 2
        + [pltpu.VMEM(heads.shape, jnp.float32)] * 3
        + [
            pltpu.VMEM((count, width), jnp.bfloat16),
            pltpu.VMEM((count, model), jnp.float32),
        ],
        cost_estimate=cost(
            4 * heads.size * keys + 2 * count * width * model, 6e6, heads.shape[0] * keys
        ),
        compiler_params=pltpu.CompilerParams(vmem_limit_bytes=ROOM),
        name="far",
    )(heads, *state, source, out_proj)


def norm_kernel(hidden_ref, own_ref, other_ref, gain_ref, resid_ref, normed_ref):
    half = own_ref.shape[0]
    start = pl.multiple_of(lax.axis_index("exp") * half, half)
    hidden = hidden_ref[pl.ds(start, half), :].astype(jnp.float32)
    resid = hidden + own_ref[...] + other_ref[...].astype(jnp.float32)
    inverse = lax.rsqrt(jnp.mean(resid * resid, axis=1, keepdims=True) + 1e-06)
    resid_ref[...] = resid
    normed_ref[...] = (resid * inverse * gain_ref[...]).astype(jnp.bfloat16)


def norm(hidden_in, own, other, norm_gain):
    return pl.pallas_call(
        norm_kernel,
        out_shape=(
            jax.ShapeDtypeStruct(own.shape, jnp.float32),
            jax.ShapeDtypeStruct(own.shape, jnp.bfloat16),
        ),
        in_specs=[whole()] * 4,
        out_specs=(whole(),) * 2,
        cost_estimate=cost(1e6, 1e6),
        compiler_params=pltpu.CompilerParams(vmem_limit_bytes=ROOM),
        name="norm",
    )(hidden_in, own, other, norm_gain)


def share_kernel(plane, *refs):
    pieces, out_ref, turned = refs[:-2], refs[-2], refs[-1]
    me = lax.axis_index("ctx")
    experts, count = pieces[0].shape[0], pieces[0].shape[1] // 2
    half = count // 2
    start = pl.multiple_of(lax.axis_index("exp") * half, half)
    number = lax.broadcasted_iota(jnp.int32, (experts, count), 0)
    lane = lax.broadcasted_iota(jnp.int32, (count, count), 1)
    diagonal = lax.broadcasted_iota(jnp.int32, (count, count), 0) == lane
    for n, piece in enumerate(pieces):
        mix = piece[:, :count].astype(jnp.float32) + piece[:, count:].astype(jnp.float32)
        columns = jnp.zeros((count, count), jnp.float32)
        for side in range(2):
            line = jnp.sum(
                jnp.where(number == (me if side == 0 else me ^ plane), mix, 0.0), axis=0, keepdims=True
            )
            column = jnp.sum(jnp.where(diagonal, line, 0.0), axis=1, keepdims=True)
            columns = jnp.where(lane == side, column, columns)
        turned[...] = columns
        out_ref[n * half : (n + 1) * half, :] = turned[pl.ds(start, half), :]


def share(pieces, experts, plane):
    width = pieces[0].shape[1]
    count = width // 2
    specs = []
    for piece in pieces:
        block = piece.shape[0] // experts - 1
        specs.append(pl.BlockSpec((experts, width), lambda i, block=block: (block, 0)))
    rows = len(pieces) * count // 2
    return pl.pallas_call(
        functools.partial(share_kernel, plane),
        grid=(1,),
        out_shape=jax.ShapeDtypeStruct((rows, count), jnp.float32),
        in_specs=specs,
        out_specs=pl.BlockSpec((rows, count), lambda i: (0, 0)),
        scratch_shapes=[pltpu.VMEM((count, count), jnp.float32)],
        cost_estimate=cost(1e6, 4e5),
        compiler_params=pltpu.CompilerParams(vmem_limit_bytes=ROOM),
        name="columns",
    )(*pieces)


def expert_rows(share_ref, first, inputs, wide_refs, rows, hidden):
    size = inputs[0].shape[0]
    units = wide_refs[0].shape[1] // 2
    for n, ref in enumerate(inputs):
        rows[n * size : (n + 1) * size, :] = ref[...]
    for side, wide_ref in enumerate(wide_refs):
        both = jnp.dot(rows[...], wide_ref[...], preferred_element_type=jnp.float32)
        gate, upper = both[:, :units], both[:, units:]
        factor = share_ref[first * size : (first + len(inputs)) * size, side : side + 1]
        value = gate / (1.0 + jnp.exp(-gate)) * upper * factor
        hidden[:, side * units : (side + 1) * units] = value.astype(jnp.bfloat16)


def expert_sums(hidden, tall_ref, outputs):
    size = outputs[0].shape[0]
    total = jnp.dot(hidden[...], tall_ref[...], preferred_element_type=jnp.float32)
    for n, ref in enumerate(outputs):
        ref[...] = total[n * size : (n + 1) * size, :].astype(ref.dtype)


def expand_kernel(share_ref, *refs):
    inputs, wide_refs, hidden, rows = refs[:-4], refs[-4:-2], refs[-2], refs[-1]
    expert_rows(share_ref, 0, inputs, wide_refs, rows, hidden)


def expand(shares, inputs, wide):
    blocks = len(inputs)
    size, model = inputs[0].shape
    both = wide[0].shape[1]
    return pl.pallas_call(
        expand_kernel,
        out_shape=jax.ShapeDtypeStruct((blocks * size, both), jnp.bfloat16),
        in_specs=[whole()] * (3 + blocks),
        out_specs=whole(),
        scratch_shapes=[pltpu.VMEM((blocks * size, model), jnp.bfloat16)],
        cost_estimate=cost(4 * blocks * size * model * both, 4 * model * both),
        compiler_params=pltpu.CompilerParams(vmem_limit_bytes=ROOM),
        name="expand",
    )(shares, *inputs, *wide)


def contract_kernel(hidden_ref, down_ref, *refs):
    pieces, outputs, tall_ref, sems = refs[:4], refs[4:-2], refs[-2], refs[-1]
    units, core = down_ref.shape[1], lax.axis_index("exp")
    pairs = [(down_ref.at[0], tall_ref.at[:units])]
    for n, position in enumerate((core, 1 - core)):
        start = units + position * (units // 2)
        for ref in pieces[n::2]:
            size = ref.shape[0]
            step = math.gcd(size, units // 6)
            band = pl.ds(pl.multiple_of(start, step), size)
            pairs.append((ref, tall_ref.at[band]))
            start = start + size
    for copy in fetch_all(pairs, sems):
        copy.wait()
    expert_sums(hidden_ref, tall_ref, outputs)


def contract(hidden, w_down, pieces, dtypes):
    blocks = len(dtypes)
    size, model = hidden.shape[0] // blocks, w_down.shape[2]
    both = hidden.shape[1]
    return pl.pallas_call(
        contract_kernel,
        out_shape=tuple(jax.ShapeDtypeStruct((size, model), dtype) for dtype in dtypes)
        + (jax.ShapeDtypeStruct((both, model), jnp.bfloat16),),
        in_specs=[whole()] + [whole(pl.ANY)] * 5,
        out_specs=(whole(),) * (blocks + 1),
        scratch_shapes=[pltpu.SemaphoreType.DMA((5,))],
        cost_estimate=cost(2 * blocks * size * model * both, 2 * model * both),
        compiler_params=pltpu.CompilerParams(vmem_limit_bytes=ROOM),
        name="contract",
    )(hidden, w_down, *pieces)


def expert_far_kernel(first, blocks, share_ref, *refs):
    inputs, wide_refs, tall_ref = refs[:blocks], refs[blocks : blocks + 2], refs[blocks + 2]
    outputs, rows, hidden = refs[blocks + 3 : -2], refs[-2], refs[-1]
    expert_rows(share_ref, first, inputs, wide_refs, rows, hidden)
    expert_sums(hidden, tall_ref, outputs)


def experts_far(shares, inputs, wide, tall, first):
    blocks = len(inputs)
    size, model = inputs[0].shape
    both = tall.shape[0]
    return pl.pallas_call(
        functools.partial(expert_far_kernel, first, blocks),
        out_shape=(jax.ShapeDtypeStruct((size, model), jnp.bfloat16),) * blocks,
        in_specs=[whole()] * (4 + blocks),
        out_specs=(whole(),) * blocks,
        scratch_shapes=[
            pltpu.VMEM((blocks * size, model), jnp.bfloat16),
            pltpu.VMEM((blocks * size, both), jnp.bfloat16),
        ],
        cost_estimate=cost(6 * blocks * size * model * both, 6 * model * both),
        compiler_params=pltpu.CompilerParams(vmem_limit_bytes=ROOM),
        name="experts_far",
    )(shares, *inputs, *wide, tall)


def final_kernel(resid_ref, own_ref, *refs):
    keep_ref, send_ref, work = refs[-3:]
    total = own_ref[...]
    for ref in refs[:-3]:
        total = total + ref[...].astype(jnp.float32)
    work[...] = (resid_ref[...] + total).astype(jnp.bfloat16)
    half = keep_ref.shape[1]
    core = lax.axis_index("exp")
    keep_ref[...] = work[:, pl.ds(pl.multiple_of(core * half, half), half)]
    send_ref[...] = work[:, pl.ds(pl.multiple_of((1 - core) * half, half), half)]


def final(resid, own, received):
    rows, model = resid.shape
    shape = jax.ShapeDtypeStruct((rows, model // 2), jnp.bfloat16)
    return pl.pallas_call(
        final_kernel,
        out_shape=(shape, shape),
        in_specs=[whole()] * (2 + len(received)),
        out_specs=(whole(),) * 2,
        scratch_shapes=[pltpu.VMEM((rows, model), jnp.bfloat16)],
        cost_estimate=cost(1e6, 1e6),
        compiler_params=pltpu.CompilerParams(vmem_limit_bytes=ROOM),
        name="final",
    )(resid, own, *received)


def compact(
    queries,
    key_rows,
    value_rows,
    hidden_in,
    out_proj,
    norm_gain,
    expert_ids,
    gate_scores,
    w_gate,
    w_up,
    w_down,
):
    count = queries.shape[0]
    model = hidden_in.shape[1]
    ctx = lax.axis_size("ctx")
    plane = math.isqrt(ctx)
    planes = ctx // plane
    away = 2 * plane


    def flip(value, mask):
        return lax.ppermute(value, "ctx", [(i, i ^ mask) for i in range(ctx)])

    def upward(value, step):
        return lax.ppermute(value, "ctx", [(i, i + step) for i in range(ctx - step)])

    def across(value):
        return lax.ppermute(value, "exp", [(0, 1), (1, 0)])

    mates = range(1, plane)
    rows, mixed = pack(key_rows, value_rows, expert_ids, gate_scores, w_gate.shape[0] * ctx)
    column = [
        flip(mixed, away)
        if step == 2
        else upward(rows, step * plane)
        for step in range(1, planes)
    ]
    level = [flip(mixed, mate) for mate in mates]
    joined = join(column, count)
    corner = [flip(joined, mate) for mate in mates]

    def half_flip(value, side):
        pairs = [(2 * i + side, 2 * (i ^ plane) + side) for i in range(ctx)]
        return lax.ppermute(value, ("ctx", "exp"), pairs)

    gate_swap = half_flip(w_gate[0], 0)
    up_swap = half_flip(w_up[0], 1)
    tall_swap = [flip(piece, plane) for piece in cut(w_down)]

    heads = turn(queries)
    state = near(heads, [mixed] + level, joined, plane)
    state = more(heads, state, corner[:-1], plane)
    own, other = far(heads, state, corner[-1], out_proj, plane)
    resid, normed = norm(hidden_in, own, across(other), norm_gain.reshape(1, model))
    wide_swap = merge(gate_swap, up_swap)
    wide = stack(w_gate, w_up, wide_swap, across(wide_swap))
    shares = share([mixed] + level + [joined] + corner, w_gate.shape[0] * ctx, plane)
    opposite = flip(normed, away)
    level_rows = [flip(normed, mate) for mate in mates]
    corner_rows = [flip(opposite, mate) for mate in mates]
    f32, bf16 = jnp.float32, jnp.bfloat16
    hidden = expand(shares, [normed] + level_rows + [opposite], wide)
    pieces = [value for piece in tall_swap for value in (piece, across(piece))]
    *near_out, tall = contract(
        hidden, w_down, pieces, [f32] + [bf16] * len(mates) + [f32]
    )
    far_out = experts_far(shares, corner_rows, wide, tall, plane + 1)
    passed = [flip(value, mate) for value, mate in zip(far_out, mates)]
    direct = [flip(value, mate) for value, mate in zip(near_out[1:plane], mates)]
    last = flip(gather_sum(near_out[plane], passed), away)
    keep, send = final(resid, near_out[0], direct + [last])
    return assemble(keep, across(send))


def gather_sum_kernel(own_ref, *refs):
    total = own_ref[...]
    for ref in refs[:-1]:
        total = total + ref[...].astype(jnp.float32)
    refs[-1][...] = total.astype(jnp.bfloat16)


def gather_sum(own, received):
    return pl.pallas_call(
        gather_sum_kernel,
        out_shape=jax.ShapeDtypeStruct(own.shape, jnp.bfloat16),
        in_specs=[whole()] * (1 + len(received)),
        out_specs=whole(),
        cost_estimate=cost(1e5, 8e5),
        compiler_params=pltpu.CompilerParams(vmem_limit_bytes=ROOM),
        name="gather_sum",
    )(own, *received)


def assemble_kernel(keep_ref, received_ref, out_ref):
    half = keep_ref.shape[0]
    core = lax.axis_index("exp")
    out_ref[pl.ds(pl.multiple_of(core * half, half), half), :] = keep_ref[...]
    out_ref[pl.ds(pl.multiple_of((1 - core) * half, half), half), :] = received_ref[...]


def assemble(keep, received):
    return pl.pallas_call(
        assemble_kernel,
        out_shape=jax.ShapeDtypeStruct((2 * keep.shape[0], keep.shape[1]), keep.dtype),
        in_specs=[whole()] * 2,
        out_specs=whole(),
        cost_estimate=cost(1e5, 3e5),
        compiler_params=pltpu.CompilerParams(vmem_limit_bytes=ROOM),
        name="assemble",
    )(keep, received)


def fits_compact(queries, key_rows, expert_ids, w_gate):
    ctx = lax.axis_size("ctx")
    plane = math.isqrt(ctx)
    return (
        plane * plane == ctx
        and plane == 4
        and lax.axis_size("exp") == 2
        and w_gate.shape[0] == 1
        and ctx <= 2 * expert_ids.shape[1]
        and key_rows.shape == (HEAD, HEAD)
        and queries.shape[0] == HEAD
    )


def attend(queries, key_rows, value_rows, first):
    token_count = queries.shape[0]
    kv_heads = key_rows.shape[1] // 128
    q_heads = queries.shape[1] // 128
    group = q_heads // kv_heads
    grouped = queries.reshape(token_count, kv_heads, group, 128)
    query_pos = first + jnp.arange(token_count, dtype=jnp.int32)
    last_pos = first + token_count - 1
    scale = 128 ** (-0.5)
    shape_rows = (kv_heads, group, token_count)
    start_state = (
        jnp.full(shape_rows, -1e30, jnp.float32),
        jnp.zeros(shape_rows, jnp.float32),
        jnp.zeros(shape_rows + (128,), jnp.float32),
    )
    key_piece = lax.all_gather(key_rows, "ctx", axis=0, tiled=True)
    value_piece = lax.all_gather(value_rows, "ctx", axis=0, tiled=True)
    count = key_piece.shape[0]
    width = math.gcd(count, 512)

    def step(block_index, state):
        offset = block_index * width

        def compute(inner):
            running_max, running_sum, accum = inner
            key_block = lax.dynamic_slice_in_dim(key_piece, block_index * width, width, 0).reshape(
                width, kv_heads, 128
            )
            value_block = lax.dynamic_slice_in_dim(
                value_piece, block_index * width, width, 0
            ).reshape(width, kv_heads, 128)
            scores = (
                jnp.einsum("tkgd,skd->kgts", grouped, key_block, preferred_element_type=jnp.float32)
                * scale
            )
            key_pos = offset + jnp.arange(width, dtype=jnp.int32)
            allowed = key_pos[None, :] <= query_pos[:, None]
            scores = jnp.where(allowed, scores, -jnp.inf)
            new_max = jnp.maximum(running_max, jnp.max(scores, axis=-1))
            factor = jnp.exp(running_max - new_max)
            weights = jnp.exp(scores - new_max[..., None])
            new_sum = running_sum * factor + jnp.sum(weights, axis=-1)
            product = jnp.einsum(
                "kgts,skd->kgtd",
                weights.astype(jnp.bfloat16),
                value_block,
                preferred_element_type=jnp.float32,
            )
            return (new_max, new_sum, accum * factor[..., None] + product)

        return lax.cond(offset <= last_pos, compute, lambda inner: inner, state)

    _, total, accum = lax.fori_loop(0, count // width, step, start_state)
    output = accum / total[..., None]
    return (
        jnp.transpose(output, (2, 0, 1, 3)).reshape(token_count, q_heads * 128).astype(jnp.bfloat16)
    )


def place_rows(expert_ids, sent_rows, capacity, expert_count):
    top_count = expert_ids.shape[1]
    flat_ids = expert_ids.reshape(-1)
    onehot = (flat_ids[:, None] == jnp.arange(expert_count, dtype=jnp.int32)[None, :]).astype(
        jnp.int32
    )
    earlier = jnp.cumsum(onehot, axis=0) - onehot
    slot_index = jnp.sum(earlier * onehot, axis=1)
    destination = flat_ids * capacity + slot_index
    copies = jnp.repeat(sent_rows, top_count, axis=0)
    buffer = (
        jnp.zeros((expert_count * capacity, sent_rows.shape[1]), sent_rows.dtype)
        .at[destination]
        .set(copies)
    )
    return (buffer.reshape(expert_count, 2, capacity // 2, sent_rows.shape[1]), destination)


def per_device(
    queries,
    key_rows,
    value_rows,
    hidden_in,
    out_proj,
    norm_gain,
    expert_ids,
    gate_scores,
    w_gate,
    w_up,
    w_down,
):
    if fits_compact(queries, key_rows, expert_ids, w_gate):
        return compact(
            queries, key_rows, value_rows, hidden_in, out_proj, norm_gain,
            expert_ids, gate_scores, w_gate, w_up, w_down,
        )
    token_count = queries.shape[0]
    model_width = hidden_in.shape[1]
    half_width = model_width // 2
    ctx_size = lax.axis_size("ctx")
    local_experts = w_gate.shape[0]
    expert_count = local_experts * ctx_size
    top_count = expert_ids.shape[1]
    capacity = 2 * (
        min(token_count, max(2, 3 * token_count * top_count // (2 * expert_count))) // 2
    )
    half_cap = capacity // 2
    first = lax.axis_index("ctx") * token_count
    core = lax.axis_index("exp")
    side_start = core * half_width
    attended = attend(queries, key_rows, value_rows, first)
    head_part = jnp.dot(attended, out_proj, preferred_element_type=jnp.float32)
    attn_full = lax.psum(head_part.astype(jnp.bfloat16), "exp").astype(jnp.float32)
    resid = hidden_in.astype(jnp.float32) + attn_full
    inverse = lax.rsqrt(jnp.mean(resid * resid, axis=1, keepdims=True) + 1e-06)
    sent_rows = (resid * inverse * norm_gain[None, :]).astype(jnp.bfloat16)
    resid_half = lax.dynamic_slice_in_dim(resid, side_start, half_width, 1)
    buffer, destination = place_rows(expert_ids, sent_rows, capacity, expert_count)
    own_slots = lax.dynamic_slice_in_dim(buffer, core, 1, 1)
    grouped = lax.all_to_all(own_slots, "ctx", split_axis=0, concat_axis=0, tiled=True)
    gate = jnp.einsum("sxmd,xdf->sxmf", grouped, w_gate, preferred_element_type=jnp.float32)
    upper = jnp.einsum("sxmd,xdf->sxmf", grouped, w_up, preferred_element_type=jnp.float32)
    hidden = (jax.nn.silu(gate) * upper).astype(jnp.bfloat16)
    partial_value = jnp.einsum(
        "sxmf,xfd->sxmd", hidden, w_down, preferred_element_type=jnp.float32
    ).astype(jnp.bfloat16)
    returned = lax.all_to_all(partial_value, "ctx", split_axis=0, concat_axis=0, tiled=True)
    flat_back = returned.reshape(expert_count * half_cap, model_width)
    slot_of = destination % capacity
    expert_of = destination // capacity
    owned = slot_of // half_cap == core
    local_index = jnp.where(owned, expert_of * half_cap + slot_of - core * half_cap, 0)
    picked = flat_back[local_index].astype(jnp.float32)
    mixing = (gate_scores / jnp.sum(gate_scores, axis=1, keepdims=True)).reshape(-1)
    mixing = jnp.where(owned, mixing, 0.0)
    weighted = (picked * mixing[:, None]).reshape(token_count, top_count, model_width)
    mixed_part = jnp.sum(weighted, axis=1)
    moe_half = lax.psum_scatter(
        mixed_part.astype(jnp.bfloat16), "exp", scatter_dimension=1, tiled=True
    ).astype(jnp.float32)
    return (resid_half + moe_half).astype(jnp.bfloat16)


def solution(mesh):
    placed = (
        P(("groups", "ctx"), "exp"),
        P(("groups", "ctx"), "exp"),
        P(("groups", "ctx"), "exp"),
        P(("groups", "ctx"), None),
        P("exp", None),
        P(),
        P(("groups", "ctx"), None),
        P(("groups", "ctx"), None),
        P("ctx", None, None),
        P("ctx", None, None),
        P("ctx", None, None),
    )
    return jax.shard_map(
        per_device,
        mesh=mesh,
        in_specs=placed,
        out_specs=P(("groups", "ctx"), "exp"),
        check_vma=False,
    )
```

```python
import functools
import math

import jax
import jax.numpy as jnp
from jax import lax
from jax.experimental import pallas as pl
from jax.experimental.pallas import tpu as pltpu
from jax.sharding import PartitionSpec as P


HEAD = 128
LOG2E = 1.4426950408889634
HIDE = -1e30
ROOM = 20 << 20
GROUP = 512


def whole(memory_space=pltpu.VMEM):
    return pl.BlockSpec(memory_space=memory_space)


def cost(flops, size, exps=0):
    return pl.CostEstimate(flops=int(flops), bytes_accessed=int(size), transcendentals=int(exps))


def fetch_all(pairs, sems):
    copies = [
        pltpu.make_async_copy(source, target, sems.at[n])
        for n, (source, target) in enumerate(pairs)
    ]
    for copy in copies:
        copy.start()
    return copies


def held(value):
    return pltpu.with_memory_space_constraint(value, pltpu.HBM)


def pack_kernel(key_ref, value_ref, ids_ref, score_ref, rows_ref, mixed_ref, both, ids, score, sems):
    count, width = key_ref.shape
    copies = fetch_all(
        [
            (key_ref, both.at[:, :width]),
            (value_ref, both.at[:, width:]),
            (ids_ref, ids),
            (score_ref, score),
        ],
        sems,
    )
    for copy in copies:
        copy.wait()
    rows_ref[...] = both[...]
    mixed_ref[:count, :] = both[...]
    experts = mixed_ref.shape[0] - count
    mix = score[...] / jnp.sum(score[...], axis=0, keepdims=True)
    number = lax.broadcasted_iota(jnp.int32, (experts, count), 0)
    turned = jnp.zeros((experts, count), jnp.float32)
    for k in range(ids.shape[0]):
        turned = turned + jnp.where(number == ids[k : k + 1, :], mix[k : k + 1, :], 0.0)
    high = turned.astype(jnp.bfloat16)
    low = (turned - high.astype(jnp.float32)).astype(jnp.bfloat16)
    mixed_ref[count:, :] = jnp.concatenate([high, low], axis=1)


def pack(key_rows, value_rows, expert_ids, gate_scores, experts):
    count, width = key_rows.shape
    top = expert_ids.shape[1]
    return pl.pallas_call(
        pack_kernel,
        out_shape=(
            jax.ShapeDtypeStruct((count, 2 * width), jnp.bfloat16),
            jax.ShapeDtypeStruct((count + experts, 2 * width), jnp.bfloat16),
        ),
        in_specs=[whole(pltpu.HBM)] * 4,
        out_specs=(whole(), whole()),
        scratch_shapes=[
            pltpu.VMEM((count, 2 * width), jnp.bfloat16),
            pltpu.VMEM((top, count), jnp.int32),
            pltpu.VMEM((top, count), jnp.float32),
            pltpu.SemaphoreType.DMA((4,)),
        ],
        cost_estimate=cost(1e5, 3e5),
        compiler_params=pltpu.CompilerParams(vmem_limit_bytes=ROOM),
        name="pack",
    )(*[held(value) for value in (key_rows, value_rows, expert_ids.T, gate_scores.T)])


def cut_kernel(down_ref, first_ref, second_ref, sems):
    size = first_ref.shape[0]
    half = size + second_ref.shape[0]
    start = lax.axis_index("exp") * half
    first = pl.ds(pl.multiple_of(start, size), size)
    second = pl.ds(pl.multiple_of(start + size, size), half - size)
    pairs = [(down_ref.at[0, first], first_ref), (down_ref.at[0, second], second_ref)]
    for copy in fetch_all(pairs, sems):
        copy.wait()


def cut(w_down):
    _, units, model = w_down.shape
    size = units // 6
    return pl.pallas_call(
        cut_kernel,
        out_shape=(
            jax.ShapeDtypeStruct((size, model), w_down.dtype),
            jax.ShapeDtypeStruct((2 * size, model), w_down.dtype),
        ),
        in_specs=[whole(pl.ANY)],
        out_specs=(whole(),) * 2,
        scratch_shapes=[pltpu.SemaphoreType.DMA((2,))],
        cost_estimate=cost(1e3, 1e6),
        compiler_params=pltpu.CompilerParams(vmem_limit_bytes=ROOM),
        name="cut",
    )(held(w_down))


def merge_kernel(first_ref, second_ref, out_ref):
    out_ref[...] = first_ref[...] + second_ref[...]


def merge(first, second):
    pair = [pltpu.with_memory_space_constraint(value, pltpu.VMEM) for value in (first, second)]
    return pl.pallas_call(
        merge_kernel,
        out_shape=jax.ShapeDtypeStruct(first.shape, first.dtype),
        in_specs=[whole()] * 2,
        out_specs=whole(),
        cost_estimate=cost(1e5, 3e6),
        compiler_params=pltpu.CompilerParams(vmem_limit_bytes=ROOM),
        name="merge",
    )(*pair)


def stack_kernel(gate_ref, up_ref, mine_ref, other_ref, own_wide, swapped_wide, sems):
    units, core = gate_ref.shape[2], lax.axis_index("exp")
    mine = pl.ds(pl.multiple_of(core * units, units), units)
    other = pl.ds(pl.multiple_of((1 - core) * units, units), units)
    pairs = [
        (gate_ref.at[0], own_wide.at[:, :units]),
        (up_ref.at[0], own_wide.at[:, units:]),
        (mine_ref, swapped_wide.at[:, mine]),
        (other_ref, swapped_wide.at[:, other]),
    ]
    for copy in fetch_all(pairs, sems):
        copy.wait()


def stack(w_gate, w_up, mine, other):
    _, model, units = w_gate.shape
    return pl.pallas_call(
        stack_kernel,
        out_shape=(jax.ShapeDtypeStruct((model, 2 * units), jnp.bfloat16),) * 2,
        in_specs=[whole(pl.ANY)] * 4,
        out_specs=(whole(),) * 2,
        scratch_shapes=[pltpu.SemaphoreType.DMA((4,))],
        cost_estimate=cost(1e5, 6e6),
        compiler_params=pltpu.CompilerParams(vmem_limit_bytes=ROOM),
        name="stack",
    )(w_gate, w_up, mine, other)


def join_kernel(count, *refs):
    out_ref = refs[-1]
    tail = None
    for n, ref in enumerate(refs[:-1]):
        out_ref[n * count : (n + 1) * count, :] = ref[:count, :]
        if ref.shape[0] > count:
            tail = ref
    out_ref[(len(refs) - 1) * count :, :] = tail[count:, :]


def join(parts, count):
    total = sum(part.shape[0] for part in parts)
    return pl.pallas_call(
        functools.partial(join_kernel, count),
        out_shape=jax.ShapeDtypeStruct((total, parts[0].shape[1]), parts[0].dtype),
        in_specs=[whole()] * len(parts),
        out_specs=whole(),
        cost_estimate=cost(1e5, 4e5),
        compiler_params=pltpu.CompilerParams(vmem_limit_bytes=ROOM),
        name="join",
    )(*parts)


def soften(query, keys, values, biases, state):
    scale = HEAD ** (-0.5) * LOG2E
    scores = lax.dot_general(
        query, keys, (((1,), (1,)), ((), ())), preferred_element_type=jnp.float32
    )
    pieces = [scores[:, n * HEAD : (n + 1) * HEAD] for n in range(keys.shape[0] // HEAD)]
    if biases is not None:
        pieces = [piece + bias for piece, bias in zip(pieces, biases)]
    peak = functools.reduce(jnp.maximum, pieces)
    peak = jnp.max(peak, axis=1, keepdims=True)
    if state is not None:
        peak = jnp.maximum(peak, state[0][:, :1])
    weights = [jnp.exp2((piece - peak) * scale) for piece in pieces]
    total = functools.reduce(jnp.add, weights)
    product = jnp.dot(
        jnp.concatenate([w.astype(jnp.bfloat16) for w in weights], axis=1),
        values,
        preferred_element_type=jnp.float32,
    )
    if state is not None:
        factor = jnp.exp2((state[0][:, :1] - peak) * scale)
        total = total + state[1] * factor
        product = product + state[2] * factor
    return peak, total, product


def near_kernel(plane, heads_ref, *refs):
    sources, column_ref = refs[:plane], refs[plane]
    peak_ref, total_ref, sum_ref, keys, values = refs[plane + 1 :]
    count = HEAD
    layers = column_ref.shape[0] // count
    for n, ref in enumerate(sources):
        keys[n * count : (n + 1) * count, :] = ref[:count, :HEAD]
        values[n * count : (n + 1) * count, :] = ref[:count, HEAD:]
    keys[plane * count :, :] = column_ref[: layers * count, :HEAD]
    values[plane * count :, :] = column_ref[: layers * count, HEAD:]
    me = lax.axis_index("ctx")
    row = lax.broadcasted_iota(jnp.int32, (GROUP, count), 0) % count
    number = lax.broadcasted_iota(jnp.int32, (GROUP, count), 1)
    biases = [jnp.where(number <= row, 0.0, HIDE)]
    for step in range(1, plane):
        biases.append(jnp.where((me ^ step) < me, 0.0, HIDE))
    for step in range(1, layers + 1):
        biases.append(jnp.where(me >= step * plane, 0.0, HIDE))
    for start in range(0, heads_ref.shape[0], GROUP):
        part = slice(start, start + GROUP)
        peak, total, product = soften(heads_ref[part], keys[...], values[...], biases, None)
        peak_ref[part] = jnp.broadcast_to(peak, (GROUP, HEAD))
        total_ref[part] = total
        sum_ref[part] = product


def turn_kernel(query_ref, heads_ref, sems):
    count = query_ref.shape[0]
    pairs = []
    for head in range(query_ref.shape[1] // HEAD):
        part = slice(head * count, (head + 1) * count)
        pairs.append((query_ref.at[:, head * HEAD : (head + 1) * HEAD], heads_ref.at[part]))
    for copy in fetch_all(pairs, sems):
        copy.wait()


def turn(queries):
    count, width = queries.shape
    return pl.pallas_call(
        turn_kernel,
        out_shape=jax.ShapeDtypeStruct((count * width // HEAD, HEAD), queries.dtype),
        in_specs=[whole(pl.ANY)],
        out_specs=whole(),
        scratch_shapes=[pltpu.SemaphoreType.DMA((width // HEAD,))],
        cost_estimate=cost(1e5, 1e6),
        compiler_params=pltpu.CompilerParams(vmem_limit_bytes=ROOM),
        name="turn",
    )(held(queries))


def near(heads, sources, column, plane):
    shape = jax.ShapeDtypeStruct(heads.shape, jnp.float32)
    keys = (plane + column.shape[0] // HEAD) * HEAD
    return pl.pallas_call(
        functools.partial(near_kernel, plane),
        out_shape=(shape,) * 3,
        in_specs=[whole()] * (2 + len(sources)),
        out_specs=(whole(),) * 3,
        scratch_shapes=[pltpu.VMEM((keys, HEAD), jnp.bfloat16)] * 2,
        cost_estimate=cost(4 * heads.size * keys, 4e6, heads.shape[0] * keys),
        compiler_params=pltpu.CompilerParams(vmem_limit_bytes=ROOM),
        name="near",
    )(heads, *sources, column)


def extend(plane, query_ref, state, sources, keys, values, out):
    count = HEAD
    layers = sources[0].shape[0] // count
    height = lax.axis_index("ctx") // plane

    @pl.when(height == 0)
    def _():
        for source, target in zip(state, out):
            target[...] = source[...]

    for used in range(1, layers + 1):

        @pl.when(height == used)
        def _(used=used):
            span = used * count
            for n, ref in enumerate(sources):
                keys[n * span : (n + 1) * span, :] = ref[:span, :HEAD]
                values[n * span : (n + 1) * span, :] = ref[:span, HEAD:]
            size = len(sources) * span
            for start in range(0, query_ref.shape[0], GROUP):
                part = slice(start, start + GROUP)
                peak, total, product = soften(
                    query_ref[part],
                    keys[:size],
                    values[:size],
                    None,
                    [ref[part] for ref in state],
                )
                out[0][part] = jnp.broadcast_to(peak, (GROUP, HEAD))
                out[1][part] = total
                out[2][part] = product


def more_kernel(plane, steps, query_ref, *refs):
    state, sources, refs = refs[:3], refs[3 : 3 + steps], refs[3 + steps :]
    extend(plane, query_ref, state, sources, refs[3], refs[4], refs[:3])


def more(heads, state, sources, plane):
    shape = jax.ShapeDtypeStruct(heads.shape, jnp.float32)
    keys = len(sources) * (sources[0].shape[0] // HEAD) * HEAD
    return pl.pallas_call(
        functools.partial(more_kernel, plane, len(sources)),
        out_shape=(shape,) * 3,
        in_specs=[whole()] * (4 + len(sources)),
        out_specs=(whole(),) * 3,
        scratch_shapes=[pltpu.VMEM((keys, HEAD), jnp.bfloat16)] * 2,
        cost_estimate=cost(4 * heads.size * keys, 4e6, heads.shape[0] * keys),
        compiler_params=pltpu.CompilerParams(vmem_limit_bytes=ROOM),
        name="more",
    )(heads, *state, *sources)


def far_kernel(plane, query_ref, peak_ref, total_ref, sum_ref, source_ref, *refs):
    weight_ref, own_ref, other_ref, keys, values, peak, total, product, attended, result = refs
    state, work = (peak_ref, total_ref, sum_ref), (peak, total, product)
    extend(plane, query_ref, state, (source_ref,), keys, values, work)
    count = attended.shape[0]
    core = lax.axis_index("exp")
    for head in range(query_ref.shape[0] // count):
        part = slice(head * count, (head + 1) * count)
        denom = jnp.sum(total[part], axis=1, keepdims=True)
        attended[:, head * HEAD : (head + 1) * HEAD] = (product[part] / denom).astype(jnp.bfloat16)
    result[...] = jnp.dot(attended[...], weight_ref[...], preferred_element_type=jnp.float32)
    half = count // 2
    own_ref[...] = result[pl.ds(pl.multiple_of(core * half, half), half), :]
    other = result[pl.ds(pl.multiple_of((1 - core) * half, half), half), :]
    other_ref[...] = other.astype(jnp.bfloat16)


def far(heads, state, source, out_proj, plane):
    width, model = out_proj.shape
    count = heads.size // width
    keys = source.shape[0] // HEAD * HEAD
    return pl.pallas_call(
        functools.partial(far_kernel, plane),
        out_shape=(
            jax.ShapeDtypeStruct((count // 2, model), jnp.float32),
            jax.ShapeDtypeStruct((count // 2, model), jnp.bfloat16),
        ),
        in_specs=[whole()] * 6,
        out_specs=(whole(),) * 2,
        scratch_shapes=[pltpu.VMEM((keys, HEAD), jnp.bfloat16)] * 2
        + [pltpu.VMEM(heads.shape, jnp.float32)] * 3
        + [
            pltpu.VMEM((count, width), jnp.bfloat16),
            pltpu.VMEM((count, model), jnp.float32),
        ],
        cost_estimate=cost(
            4 * heads.size * keys + 2 * count * width * model, 6e6, heads.shape[0] * keys
        ),
        compiler_params=pltpu.CompilerParams(vmem_limit_bytes=ROOM),
        name="far",
    )(heads, *state, source, out_proj)


def norm_kernel(hidden_ref, own_ref, other_ref, gain_ref, resid_ref, normed_ref):
    half = own_ref.shape[0]
    start = pl.multiple_of(lax.axis_index("exp") * half, half)
    hidden = hidden_ref[pl.ds(start, half), :].astype(jnp.float32)
    resid = hidden + own_ref[...] + other_ref[...].astype(jnp.float32)
    inverse = lax.rsqrt(jnp.mean(resid * resid, axis=1, keepdims=True) + 1e-06)
    resid_ref[...] = resid
    normed_ref[...] = (resid * inverse * gain_ref[...]).astype(jnp.bfloat16)


def norm(hidden_in, own, other, norm_gain):
    return pl.pallas_call(
        norm_kernel,
        out_shape=(
            jax.ShapeDtypeStruct(own.shape, jnp.float32),
            jax.ShapeDtypeStruct(own.shape, jnp.bfloat16),
        ),
        in_specs=[whole()] * 4,
        out_specs=(whole(),) * 2,
        cost_estimate=cost(1e6, 1e6),
        compiler_params=pltpu.CompilerParams(vmem_limit_bytes=ROOM),
        name="norm",
    )(hidden_in, own, other, norm_gain)


def share_kernel(plane, *refs):
    pieces, out_ref, turned = refs[:-2], refs[-2], refs[-1]
    me = lax.axis_index("ctx")
    experts, count = pieces[0].shape[0], pieces[0].shape[1] // 2
    half = count // 2
    start = pl.multiple_of(lax.axis_index("exp") * half, half)
    number = lax.broadcasted_iota(jnp.int32, (experts, count), 0)
    lane = lax.broadcasted_iota(jnp.int32, (count, count), 1)
    diagonal = lax.broadcasted_iota(jnp.int32, (count, count), 0) == lane
    for n, piece in enumerate(pieces):
        mix = piece[:, :count].astype(jnp.float32) + piece[:, count:].astype(jnp.float32)
        columns = jnp.zeros((count, count), jnp.float32)
        for side in range(2):
            line = jnp.sum(
                jnp.where(number == (me if side == 0 else me ^ plane), mix, 0.0), axis=0, keepdims=True
            )
            column = jnp.sum(jnp.where(diagonal, line, 0.0), axis=1, keepdims=True)
            columns = jnp.where(lane == side, column, columns)
        turned[...] = columns
        out_ref[n * half : (n + 1) * half, :] = turned[pl.ds(start, half), :]


def share(pieces, experts, plane):
    width = pieces[0].shape[1]
    count = width // 2
    specs = []
    for piece in pieces:
        block = piece.shape[0] // experts - 1
        specs.append(pl.BlockSpec((experts, width), lambda i, block=block: (block, 0)))
    rows = len(pieces) * count // 2
    return pl.pallas_call(
        functools.partial(share_kernel, plane),
        grid=(1,),
        out_shape=jax.ShapeDtypeStruct((rows, count), jnp.float32),
        in_specs=specs,
        out_specs=pl.BlockSpec((rows, count), lambda i: (0, 0)),
        scratch_shapes=[pltpu.VMEM((count, count), jnp.float32)],
        cost_estimate=cost(1e6, 4e5),
        compiler_params=pltpu.CompilerParams(vmem_limit_bytes=ROOM),
        name="columns",
    )(*pieces)


def expert_rows(share_ref, first, inputs, wide_refs, rows, hidden):
    size = inputs[0].shape[0]
    units = wide_refs[0].shape[1] // 2
    for n, ref in enumerate(inputs):
        rows[n * size : (n + 1) * size, :] = ref[...]
    for side, wide_ref in enumerate(wide_refs):
        both = jnp.dot(rows[...], wide_ref[...], preferred_element_type=jnp.float32)
        gate, upper = both[:, :units], both[:, units:]
        factor = share_ref[first * size : (first + len(inputs)) * size, side : side + 1]
        value = gate / (1.0 + jnp.exp(-gate)) * upper * factor
        hidden[:, side * units : (side + 1) * units] = value.astype(jnp.bfloat16)


def expert_sums(hidden, tall_ref, outputs):
    size = outputs[0].shape[0]
    total = jnp.dot(hidden[...], tall_ref[...], preferred_element_type=jnp.float32)
    for n, ref in enumerate(outputs):
        ref[...] = total[n * size : (n + 1) * size, :].astype(ref.dtype)


def expand_kernel(share_ref, *refs):
    inputs, wide_refs, hidden, rows = refs[:-4], refs[-4:-2], refs[-2], refs[-1]
    expert_rows(share_ref, 0, inputs, wide_refs, rows, hidden)


def expand(shares, inputs, wide):
    blocks = len(inputs)
    size, model = inputs[0].shape
    both = wide[0].shape[1]
    return pl.pallas_call(
        expand_kernel,
        out_shape=jax.ShapeDtypeStruct((blocks * size, both), jnp.bfloat16),
        in_specs=[whole()] * (3 + blocks),
        out_specs=whole(),
        scratch_shapes=[pltpu.VMEM((blocks * size, model), jnp.bfloat16)],
        cost_estimate=cost(4 * blocks * size * model * both, 4 * model * both),
        compiler_params=pltpu.CompilerParams(vmem_limit_bytes=ROOM),
        name="expand",
    )(shares, *inputs, *wide)


def contract_kernel(hidden_ref, down_ref, *refs):
    pieces, outputs, tall_ref, sems = refs[:4], refs[4:-2], refs[-2], refs[-1]
    units, core = down_ref.shape[1], lax.axis_index("exp")
    pairs = [(down_ref.at[0], tall_ref.at[:units])]
    for n, position in enumerate((core, 1 - core)):
        start = units + position * (units // 2)
        for ref in pieces[n::2]:
            size = ref.shape[0]
            step = math.gcd(size, units // 6)
            band = pl.ds(pl.multiple_of(start, step), size)
            pairs.append((ref, tall_ref.at[band]))
            start = start + size
    for copy in fetch_all(pairs, sems):
        copy.wait()
    expert_sums(hidden_ref, tall_ref, outputs)


def contract(hidden, w_down, pieces, dtypes):
    blocks = len(dtypes)
    size, model = hidden.shape[0] // blocks, w_down.shape[2]
    both = hidden.shape[1]
    return pl.pallas_call(
        contract_kernel,
        out_shape=tuple(jax.ShapeDtypeStruct((size, model), dtype) for dtype in dtypes)
        + (jax.ShapeDtypeStruct((both, model), jnp.bfloat16),),
        in_specs=[whole()] + [whole(pl.ANY)] * 5,
        out_specs=(whole(),) * (blocks + 1),
        scratch_shapes=[pltpu.SemaphoreType.DMA((5,))],
        cost_estimate=cost(2 * blocks * size * model * both, 2 * model * both),
        compiler_params=pltpu.CompilerParams(vmem_limit_bytes=ROOM),
        name="contract",
    )(hidden, w_down, *pieces)


def expert_far_kernel(first, blocks, share_ref, *refs):
    inputs, wide_refs, tall_ref = refs[:blocks], refs[blocks : blocks + 2], refs[blocks + 2]
    outputs, rows, hidden = refs[blocks + 3 : -2], refs[-2], refs[-1]
    expert_rows(share_ref, first, inputs, wide_refs, rows, hidden)
    expert_sums(hidden, tall_ref, outputs)


def experts_far(shares, inputs, wide, tall, first):
    blocks = len(inputs)
    size, model = inputs[0].shape
    both = tall.shape[0]
    return pl.pallas_call(
        functools.partial(expert_far_kernel, first, blocks),
        out_shape=(jax.ShapeDtypeStruct((size, model), jnp.bfloat16),) * blocks,
        in_specs=[whole()] * (4 + blocks),
        out_specs=(whole(),) * blocks,
        scratch_shapes=[
            pltpu.VMEM((blocks * size, model), jnp.bfloat16),
            pltpu.VMEM((blocks * size, both), jnp.bfloat16),
        ],
        cost_estimate=cost(6 * blocks * size * model * both, 6 * model * both),
        compiler_params=pltpu.CompilerParams(vmem_limit_bytes=ROOM),
        name="experts_far",
    )(shares, *inputs, *wide, tall)


def final_kernel(resid_ref, own_ref, *refs):
    keep_ref, send_ref, work = refs[-3:]
    total = own_ref[...]
    for ref in refs[:-3]:
        total = total + ref[...].astype(jnp.float32)
    work[...] = (resid_ref[...] + total).astype(jnp.bfloat16)
    half = keep_ref.shape[1]
    core = lax.axis_index("exp")
    keep_ref[...] = work[:, pl.ds(pl.multiple_of(core * half, half), half)]
    send_ref[...] = work[:, pl.ds(pl.multiple_of((1 - core) * half, half), half)]


def final(resid, own, received):
    rows, model = resid.shape
    shape = jax.ShapeDtypeStruct((rows, model // 2), jnp.bfloat16)
    return pl.pallas_call(
        final_kernel,
        out_shape=(shape, shape),
        in_specs=[whole()] * (2 + len(received)),
        out_specs=(whole(),) * 2,
        scratch_shapes=[pltpu.VMEM((rows, model), jnp.bfloat16)],
        cost_estimate=cost(1e6, 1e6),
        compiler_params=pltpu.CompilerParams(vmem_limit_bytes=ROOM),
        name="final",
    )(resid, own, *received)


def compact(
    queries,
    key_rows,
    value_rows,
    hidden_in,
    out_proj,
    norm_gain,
    expert_ids,
    gate_scores,
    w_gate,
    w_up,
    w_down,
):
    count = queries.shape[0]
    model = hidden_in.shape[1]
    ctx = lax.axis_size("ctx")
    plane = math.isqrt(ctx)
    planes = ctx // plane
    away = 2 * plane


    def flip(value, mask):
        return lax.ppermute(value, "ctx", [(i, i ^ mask) for i in range(ctx)])

    def upward(value, step):
        return lax.ppermute(value, "ctx", [(i, i + step) for i in range(ctx - step)])

    def across(value):
        return lax.ppermute(value, "exp", [(0, 1), (1, 0)])

    mates = range(1, plane)
    rows, mixed = pack(key_rows, value_rows, expert_ids, gate_scores, w_gate.shape[0] * ctx)
    column = [
        flip(mixed, away)
        if step == 2
        else upward(rows, step * plane)
        for step in range(1, planes)
    ]
    level = [flip(mixed, mate) for mate in mates]
    joined = join(column, count)
    corner = [flip(joined, mate) for mate in mates]

    def half_flip(value, side):
        pairs = [(2 * i + side, 2 * (i ^ plane) + side) for i in range(ctx)]
        return lax.ppermute(value, ("ctx", "exp"), pairs)

    gate_swap = half_flip(w_gate[0], 0)
    up_swap = half_flip(w_up[0], 1)
    tall_swap = [flip(piece, plane) for piece in cut(w_down)]

    heads = turn(queries)
    state = near(heads, [mixed] + level, joined, plane)
    state = more(heads, state, corner[:-1], plane)
    own, other = far(heads, state, corner[-1], out_proj, plane)
    resid, normed = norm(hidden_in, own, across(other), norm_gain.reshape(1, model))
    wide_swap = merge(gate_swap, up_swap)
    wide = stack(w_gate, w_up, wide_swap, across(wide_swap))
    shares = share([mixed] + level + [joined] + corner, w_gate.shape[0] * ctx, plane)
    opposite = flip(normed, away)
    level_rows = [flip(normed, mate) for mate in mates]
    corner_rows = [flip(opposite, mate) for mate in mates]
    f32, bf16 = jnp.float32, jnp.bfloat16
    hidden = expand(shares, [normed] + level_rows + [opposite], wide)
    pieces = [value for piece in tall_swap for value in (piece, across(piece))]
    *near_out, tall = contract(
        hidden, w_down, pieces, [f32] + [bf16] * len(mates) + [f32]
    )
    far_out = experts_far(shares, corner_rows, wide, tall, plane + 1)
    passed = [flip(value, mate) for value, mate in zip(far_out, mates)]
    direct = [flip(value, mate) for value, mate in zip(near_out[1:plane], mates)]
    last = flip(gather_sum(near_out[plane], passed), away)
    keep, send = final(resid, near_out[0], direct + [last])
    return assemble(keep, across(send))


def gather_sum_kernel(own_ref, *refs):
    total = own_ref[...]
    for ref in refs[:-1]:
        total = total + ref[...].astype(jnp.float32)
    refs[-1][...] = total.astype(jnp.bfloat16)


def gather_sum(own, received):
    return pl.pallas_call(
        gather_sum_kernel,
        out_shape=jax.ShapeDtypeStruct(own.shape, jnp.bfloat16),
        in_specs=[whole()] * (1 + len(received)),
        out_specs=whole(),
        cost_estimate=cost(1e5, 8e5),
        compiler_params=pltpu.CompilerParams(vmem_limit_bytes=ROOM),
        name="gather_sum",
    )(own, *received)


def assemble_kernel(keep_ref, received_ref, out_ref):
    half = keep_ref.shape[0]
    core = lax.axis_index("exp")
    out_ref[pl.ds(pl.multiple_of(core * half, half), half), :] = keep_ref[...]
    out_ref[pl.ds(pl.multiple_of((1 - core) * half, half), half), :] = received_ref[...]


def assemble(keep, received):
    return pl.pallas_call(
        assemble_kernel,
        out_shape=jax.ShapeDtypeStruct((2 * keep.shape[0], keep.shape[1]), keep.dtype),
        in_specs=[whole()] * 2,
        out_specs=whole(),
        cost_estimate=cost(1e5, 3e5),
        compiler_params=pltpu.CompilerParams(vmem_limit_bytes=ROOM),
        name="assemble",
    )(keep, received)


def fits_compact(queries, key_rows, expert_ids, w_gate):
    ctx = lax.axis_size("ctx")
    plane = math.isqrt(ctx)
    return (
        plane * plane == ctx
        and plane == 4
        and lax.axis_size("exp") == 2
        and w_gate.shape[0] == 1
        and ctx <= 2 * expert_ids.shape[1]
        and key_rows.shape == (HEAD, HEAD)
        and queries.shape[0] == HEAD
    )


def attend(queries, key_rows, value_rows, first):
    token_count = queries.shape[0]
    kv_heads = key_rows.shape[1] // 128
    q_heads = queries.shape[1] // 128
    group = q_heads // kv_heads
    grouped = queries.reshape(token_count, kv_heads, group, 128)
    query_pos = first + jnp.arange(token_count, dtype=jnp.int32)
    last_pos = first + token_count - 1
    scale = 128 ** (-0.5)
    shape_rows = (kv_heads, group, token_count)
    start_state = (
        jnp.full(shape_rows, -1e30, jnp.float32),
        jnp.zeros(shape_rows, jnp.float32),
        jnp.zeros(shape_rows + (128,), jnp.float32),
    )
    key_piece = lax.all_gather(key_rows, "ctx", axis=0, tiled=True)
    value_piece = lax.all_gather(value_rows, "ctx", axis=0, tiled=True)
    count = key_piece.shape[0]
    width = math.gcd(count, 512)

    def step(block_index, state):
        offset = block_index * width

        def compute(inner):
            running_max, running_sum, accum = inner
            key_block = lax.dynamic_slice_in_dim(key_piece, block_index * width, width, 0).reshape(
                width, kv_heads, 128
            )
            value_block = lax.dynamic_slice_in_dim(
                value_piece, block_index * width, width, 0
            ).reshape(width, kv_heads, 128)
            scores = (
                jnp.einsum("tkgd,skd->kgts", grouped, key_block, preferred_element_type=jnp.float32)
                * scale
            )
            key_pos = offset + jnp.arange(width, dtype=jnp.int32)
            allowed = key_pos[None, :] <= query_pos[:, None]
            scores = jnp.where(allowed, scores, -jnp.inf)
            new_max = jnp.maximum(running_max, jnp.max(scores, axis=-1))
            factor = jnp.exp(running_max - new_max)
            weights = jnp.exp(scores - new_max[..., None])
            new_sum = running_sum * factor + jnp.sum(weights, axis=-1)
            product = jnp.einsum(
                "kgts,skd->kgtd",
                weights.astype(jnp.bfloat16),
                value_block,
                preferred_element_type=jnp.float32,
            )
            return (new_max, new_sum, accum * factor[..., None] + product)

        return lax.cond(offset <= last_pos, compute, lambda inner: inner, state)

    _, total, accum = lax.fori_loop(0, count // width, step, start_state)
    output = accum / total[..., None]
    return (
        jnp.transpose(output, (2, 0, 1, 3)).reshape(token_count, q_heads * 128).astype(jnp.bfloat16)
    )


def place_rows(expert_ids, sent_rows, capacity, expert_count):
    top_count = expert_ids.shape[1]
    flat_ids = expert_ids.reshape(-1)
    onehot = (flat_ids[:, None] == jnp.arange(expert_count, dtype=jnp.int32)[None, :]).astype(
        jnp.int32
    )
    earlier = jnp.cumsum(onehot, axis=0) - onehot
    slot_index = jnp.sum(earlier * onehot, axis=1)
    destination = flat_ids * capacity + slot_index
    copies = jnp.repeat(sent_rows, top_count, axis=0)
    buffer = (
        jnp.zeros((expert_count * capacity, sent_rows.shape[1]), sent_rows.dtype)
        .at[destination]
        .set(copies)
    )
    return (buffer.reshape(expert_count, 2, capacity // 2, sent_rows.shape[1]), destination)


def per_device(
    queries,
    key_rows,
    value_rows,
    hidden_in,
    out_proj,
    norm_gain,
    expert_ids,
    gate_scores,
    w_gate,
    w_up,
    w_down,
):
    if fits_compact(queries, key_rows, expert_ids, w_gate):
        return compact(
            queries, key_rows, value_rows, hidden_in, out_proj, norm_gain,
            expert_ids, gate_scores, w_gate, w_up, w_down,
        )
    token_count = queries.shape[0]
    model_width = hidden_in.shape[1]
    half_width = model_width // 2
    ctx_size = lax.axis_size("ctx")
    local_experts = w_gate.shape[0]
    expert_count = local_experts * ctx_size
    top_count = expert_ids.shape[1]
    capacity = 2 * (
        min(token_count, max(2, 3 * token_count * top_count // (2 * expert_count))) // 2
    )
    half_cap = capacity // 2
    first = lax.axis_index("ctx") * token_count
    core = lax.axis_index("exp")
    side_start = core * half_width
    attended = attend(queries, key_rows, value_rows, first)
    head_part = jnp.dot(attended, out_proj, preferred_element_type=jnp.float32)
    attn_full = lax.psum(head_part.astype(jnp.bfloat16), "exp").astype(jnp.float32)
    resid = hidden_in.astype(jnp.float32) + attn_full
    inverse = lax.rsqrt(jnp.mean(resid * resid, axis=1, keepdims=True) + 1e-06)
    sent_rows = (resid * inverse * norm_gain[None, :]).astype(jnp.bfloat16)
    resid_half = lax.dynamic_slice_in_dim(resid, side_start, half_width, 1)
    buffer, destination = place_rows(expert_ids, sent_rows, capacity, expert_count)
    own_slots = lax.dynamic_slice_in_dim(buffer, core, 1, 1)
    grouped = lax.all_to_all(own_slots, "ctx", split_axis=0, concat_axis=0, tiled=True)
    gate = jnp.einsum("sxmd,xdf->sxmf", grouped, w_gate, preferred_element_type=jnp.float32)
    upper = jnp.einsum("sxmd,xdf->sxmf", grouped, w_up, preferred_element_type=jnp.float32)
    hidden = (jax.nn.silu(gate) * upper).astype(jnp.bfloat16)
    partial_value = jnp.einsum(
        "sxmf,xfd->sxmd", hidden, w_down, preferred_element_type=jnp.float32
    ).astype(jnp.bfloat16)
    returned = lax.all_to_all(partial_value, "ctx", split_axis=0, concat_axis=0, tiled=True)
    flat_back = returned.reshape(expert_count * half_cap, model_width)
    slot_of = destination % capacity
    expert_of = destination // capacity
    owned = slot_of // half_cap == core
    local_index = jnp.where(owned, expert_of * half_cap + slot_of - core * half_cap, 0)
    picked = flat_back[local_index].astype(jnp.float32)
    mixing = (gate_scores / jnp.sum(gate_scores, axis=1, keepdims=True)).reshape(-1)
    mixing = jnp.where(owned, mixing, 0.0)
    weighted = (picked * mixing[:, None]).reshape(token_count, top_count, model_width)
    mixed_part = jnp.sum(weighted, axis=1)
    moe_half = lax.psum_scatter(
        mixed_part.astype(jnp.bfloat16), "exp", scatter_dimension=1, tiled=True
    ).astype(jnp.float32)
    return (resid_half + moe_half).astype(jnp.bfloat16)


def solution(mesh):
    placed = (
        P(("groups", "ctx"), "exp"),
        P(("groups", "ctx"), "exp"),
        P(("groups", "ctx"), "exp"),
        P(("groups", "ctx"), None),
        P("exp", None),
        P(),
        P(("groups", "ctx"), None),
        P(("groups", "ctx"), None),
        P("ctx", None, None),
        P("ctx", None, None),
        P("ctx", None, None),
    )
    return jax.shard_map(
        per_device,
        mesh=mesh,
        in_specs=placed,
        out_specs=P(("groups", "ctx"), "exp"),
        check_vma=False,
    )
```
